32 devices in a mesh: section: 16 (over z, y, core), ctx: 2 (over x).
Axes of the slice: x: 2, y: 2, z: 4, core: 2. Of those that a mesh axis runs over, the one named last changes fastest.
Arguments:
- queries: bfloat16 [16, 256, 8192], P('section', 'ctx'), may hold values from -6 to 6
- key_states: bfloat16 [16, 256, 1024], P('section', 'ctx'), may hold values from -6 to 6
- value_states: bfloat16 [16, 256, 1024], P('section', 'ctx'), may hold values from -1.5 to 1.5
- out_grad: bfloat16 [16, 256, 8192], P('section', 'ctx'), may hold values from -6 to 6
- node_end: int32 [16, 256], P('section'), may hold values from 1 to 256, as said below
- block_list: int32 [16, 2, 2], P('section'), may hold values from 0 to 1, as said below
- block_count: int32 [16, 2], P('section'), may hold values from 1 to 2, as said below
Outputs:
- query_grads: bfloat16 [16, 256, 8192], P('section', 'ctx')
- key_grads: bfloat16 [16, 256, 1024], P('section', 'ctx')
- value_grads: bfloat16 [16, 256, 1024], P('section', 'ctx')
The draws below stay inside these ranges and needn't reach their ends.
Inputs may be any that keep to these rules, and one draw needn't show every extreme that they name: Each section packs search trees one after another, each in preorder; node_end[s, j] is one past the last node of node j's subtree, so j is an ancestor of i (or i itself) exactly when j <= i < node_end[s, j]. Row b of block_list[s] lists, in increasing order, every key block that holds an ancestor (or the node itself) of some node of query block b, and no other; b itself is always listed; entries after the first block_count[s, b] are 0. block_count[s, b] is the number of listed key blocks of query block b, at most b + 1.
All inputs are finite; a program needn't handle non-finite values.
Results may differ from the reference program's by a relative error of at most 0.0053.
Values may be sent and summed in bfloat16 or wider, within the bound.
A program may use at most 128 MiB of HBM per device.

```python
import math
import jax
import jax.numpy as jnp
from jax import lax

HEADS = 64
KV_HEADS = 8
HEAD_DIM = 128
BLK = 128
SECTIONS = 16
SEQ = 256
NBLK = 2


def tree_depths(key):
    base = jax.random.fold_in(key, 11)

    def one_section(section_index):
        section_key = jax.random.fold_in(base, section_index)
        first_key, second_key, third_key = jax.random.split(section_key, 3)
        fresh = jax.random.randint(first_key, (SEQ,), 0, 2048)
        deeper = jax.random.randint(second_key, (SEQ,), 0, 4)
        jumps = jax.random.randint(third_key, (SEQ,), 0, 1048576)
        position = jnp.arange(SEQ, dtype=jnp.int32)
        forced = section_index == 0

        def advance(carry, inputs):
            depth, floor_depth = carry
            fresh_now, deeper_now, jump_now, place = inputs
            marker = forced & (place > 0) & (place % BLK == 0)
            rooted = (place == 0) | (fresh_now == 0) & jnp.logical_not(forced)
            climbs = (deeper_now < 3) | (depth == 0) | marker
            lowered = floor_depth + 1 + jump_now % jnp.maximum(depth - floor_depth, 1)
            following = jnp.where(rooted, 0, jnp.where(climbs, depth + 1, lowered)).astype(jnp.int32)
            next_floor = jnp.where(marker, following, floor_depth).astype(jnp.int32)
            return ((following, next_floor), following)
        unused, depth = lax.scan(advance, (jnp.int32(0), jnp.int32(0)), (fresh, deeper, jumps, position))
        return depth
    return lax.map(one_section, jnp.arange(SECTIONS, dtype=jnp.int32))


def tree_tables(key):
    depth = tree_depths(key)
    position = jnp.arange(SEQ, dtype=jnp.int32)
    blocks = jnp.arange(NBLK, dtype=jnp.int32)

    def one_section(depth_row):
        later = (position[None, :] > position[:, None]) & (depth_row[None, :] <= depth_row[:, None])
        subtree_end = jnp.min(jnp.where(later, position[None, :], SEQ), axis=1).astype(jnp.int32)
        ancestry = (position[None, :] <= position[:, None]) & (position[:, None] < subtree_end[None, :])
        block_flags = jnp.any(ancestry.reshape(NBLK, BLK, NBLK, BLK), axis=(1, 3))
        ranked = jnp.argsort(jnp.where(block_flags, blocks[None, :], NBLK + blocks[None, :]), axis=1).astype(jnp.int32)
        counts = jnp.sum(block_flags.astype(jnp.int32), axis=1).astype(jnp.int32)
        block_rows = jnp.where(blocks[None, :] < counts[:, None], ranked, 0).astype(jnp.int32)
        return (subtree_end, block_rows, counts)
    return lax.map(one_section, depth)


def draw_node_end(key, part):
    return tree_tables(key)[0]


def draw_block_list(key, part):
    return tree_tables(key)[1]


def draw_block_count(key, part):
    return tree_tables(key)[2]


def draw_queries(key, part):
    shape = (SECTIONS, SEQ, KV_HEADS, HEADS // KV_HEADS, HEAD_DIM)
    base = jnp.clip(jax.random.normal(jax.random.fold_in(key, 22), shape, jnp.float32), -6.0, 6.0)
    return base.reshape(SECTIONS, SEQ, HEADS * HEAD_DIM).astype(jnp.bfloat16)


def draw_key_states(key, part):
    shape = (SECTIONS, SEQ, KV_HEADS, HEAD_DIM)
    base = jnp.clip(jax.random.normal(jax.random.fold_in(key, 23), shape, jnp.float32), -6.0, 6.0)
    return base.reshape(SECTIONS, SEQ, KV_HEADS * HEAD_DIM).astype(jnp.bfloat16)


def block_scale(stream_key, dims, pieces, least, largest):
    def one(axis_at, parts):
        draws = jax.random.uniform(jax.random.fold_in(jax.random.fold_in(stream_key, 6), axis_at), (parts,), jnp.float32, least / len(pieces), largest / len(pieces))
        return jnp.repeat(jnp.exp(draws), dims[axis_at] // parts).reshape((-1,) + (1,) * (len(dims) - axis_at - 1))

    loudness = one(*pieces[0])
    for cut in pieces[1:]:
        loudness = loudness * one(*cut)
    return loudness


def centred(key, shape, scale, bound, cuts=(), kind=jnp.bfloat16):
    result = jax.random.normal(key, shape, jnp.float32) * scale
    if len(cuts) > 0:
        result = block_scale(key, shape, cuts, -0.22, 0.18) * result
    return jnp.clip(result, min=-bound, max=bound).astype(kind)


def setup_inputs(seed: int = 0) -> dict:
    key_of = jax.random.split(jax.random.key(seed), 8)
    return {
        "queries": draw_queries(jax.random.fold_in(key_of[7], 71), 0),
        "key_states": draw_key_states(jax.random.fold_in(key_of[7], 71), 0),
        "value_states": centred(key_of[2], (SECTIONS, SEQ, KV_HEADS * HEAD_DIM), 0.25, 1.5, ((0, 16), (1, 2))),
        "out_grad": centred(key_of[3], (SECTIONS, SEQ, HEADS * HEAD_DIM), 1.0, 6.0, ((0, 16), (1, 2))),
        "node_end": draw_node_end(jax.random.fold_in(key_of[7], 71), 0),
        "block_list": draw_block_list(jax.random.fold_in(key_of[7], 71), 0),
        "block_count": draw_block_count(jax.random.fold_in(key_of[7], 71), 0),
    }


def allowed_mask(end_row, list_rows, count_row):
    position = jnp.arange(SEQ, dtype=jnp.int32)
    ancestry = (position[None, :] <= position[:, None]) & (position[:, None] < end_row[None, :])
    entries = jnp.arange(NBLK, dtype=jnp.int32)
    listed = jnp.any((list_rows[:, :, None] == entries[None, None, :]) & (entries[None, :, None] < count_row[:, None, None]), axis=1)
    spread = jnp.repeat(jnp.repeat(listed, BLK, axis=0), BLK, axis=1)
    return ancestry & spread

def group_grads(query_rows, grad_rows, key_rows, value_rows, allowed):
    row_total = query_rows.shape[0]
    scale = 1.0 / math.sqrt(HEAD_DIM)
    query_heads = query_rows.reshape(row_total, -1, HEAD_DIM).astype(jnp.float32)
    grad_heads = grad_rows.reshape(row_total, -1, HEAD_DIM).astype(jnp.float32)
    key_float = key_rows.astype(jnp.float32)
    value_float = value_rows.astype(jnp.float32)
    scores = jnp.einsum('qhd,kd->hqk', query_heads, key_float) * scale
    scores = jnp.where(allowed[None], scores, -jnp.inf)
    row_max = lax.optimization_barrier(jnp.max(scores, axis=2, keepdims=True))
    exponent = jnp.exp(scores - row_max)
    attention = exponent / lax.optimization_barrier(jnp.sum(exponent, axis=2, keepdims=True))
    attention_half = attention.astype(jnp.bfloat16)
    weight_grad = jnp.einsum('qhd,kd->hqk', grad_heads, value_float)
    row_delta = lax.optimization_barrier(jnp.sum(attention * weight_grad, axis=2, keepdims=True))
    score_grad = (attention * (weight_grad - row_delta) * scale).astype(jnp.bfloat16)
    score_float = score_grad.astype(jnp.float32)
    query_grad = jnp.einsum('hqk,kd->qhd', score_float, key_float).reshape(row_total, -1)
    key_grad = jnp.einsum('hqk,qhd->kd', score_float, query_heads)
    value_grad = jnp.einsum('hqk,qhd->kd', attention_half.astype(jnp.float32), grad_heads)
    return (query_grad, key_grad, value_grad)

def section_grads(section_inputs):
    query_all, key_all, value_all, grad_all, end_row, list_rows, count_row = section_inputs
    allowed = allowed_mask(end_row, list_rows, count_row)
    width = HEADS // KV_HEADS * HEAD_DIM
    query_parts = []
    key_parts = []
    value_parts = []
    for group_index in range(KV_HEADS):
        query_grad, key_grad, value_grad = group_grads(query_all[:, group_index * width:(group_index + 1) * width], grad_all[:, group_index * width:(group_index + 1) * width], key_all[:, group_index * HEAD_DIM:(group_index + 1) * HEAD_DIM], value_all[:, group_index * HEAD_DIM:(group_index + 1) * HEAD_DIM], allowed)
        query_parts.append(query_grad)
        key_parts.append(key_grad)
        value_parts.append(value_grad)
    return (jnp.concatenate(query_parts, axis=1).astype(jnp.bfloat16), jnp.concatenate(key_parts, axis=1).astype(jnp.bfloat16), jnp.concatenate(value_parts, axis=1).astype(jnp.bfloat16))

def reference(queries, key_states, value_states, out_grad, node_end, block_list, block_count):
    query_grad, key_grad, value_grad = lax.map(section_grads, (queries, key_states, value_states, out_grad, node_end, block_list, block_count))
    return (jnp.roll(query_grad, -1, axis=0), jnp.roll(key_grad, -1, axis=0), jnp.roll(value_grad, -1, axis=0))
```

```python
import functools
import math

import jax
import jax.numpy as jnp
from jax import lax
from jax.experimental import pallas as pl
from jax.experimental.pallas import tpu as pltpu
from jax.sharding import PartitionSpec as P

HEADS = 64
KV_HEADS = 8
HEAD_DIM = 128
BLK = 128
RATIO = HEADS // KV_HEADS
PAIR = 4
WIDTH = RATIO * HEAD_DIM

F32 = jnp.float32
BF16 = jnp.bfloat16
MESH = pl.DeviceIdType.MESH


def contract(left, right, left_dim, right_dim):
    return lax.dot_general(
        left, right, (((left_dim,), (right_dim,)), ((), ())), preferred_element_type=F32
    )


def kernel(
    section_total,
    ctx_total,
    q_hbm,
    k_hbm,
    v_hbm,
    g_hbm,
    end_hbm,
    list_hbm,
    count_hbm,
    out_q,
    out_k,
    out_v,
    q_buf,
    g_buf,
    kv_buf,
    dq_buf,
    ds_buf,
    at_buf,
    bias,
    own,
    share,
    shares_in,
    final,
    end_ref,
    list_ref,
    count_ref,
    table_sem,
    load_sem,
    kv_sem,
    kv_send,
    kv_recv,
    dq_send,
    share_send,
    share_recv,
    final_send,
    out_recv,
):
    rows = q_hbm.shape[1]
    block_total = list_hbm.shape[1]
    blocks_here = rows // BLK
    scale = 1.0 / math.sqrt(HEAD_DIM)
    section = lax.axis_index("section")
    ctx = lax.axis_index("ctx")
    before = lax.rem(section + section_total - 1, section_total)
    after = lax.rem(section + 1, section_total)

    def cols(index, width=HEAD_DIM):
        if isinstance(index, int):
            return slice(index * width, index * width + width)
        return pl.ds(pl.multiple_of(index * width, width), width)

    def block(index):
        return pl.ds(pl.multiple_of(index * rows, rows), rows)

    barrier = pltpu.get_barrier_semaphore()
    for target in (before, after):
        pl.semaphore_signal(barrier, 1, device_id={"section": target}, device_id_type=MESH)
    for step in range(1, ctx_total):
        other = lax.rem(ctx + step, ctx_total)
        pl.semaphore_signal(barrier, 1, device_id={"ctx": other}, device_id_type=MESH)

    def load(group):
        for which, source in enumerate((k_hbm, v_hbm)):
            pltpu.make_async_copy(
                source.at[0, :, cols(group)], kv_buf.at[group, which, block(ctx)], kv_sem.at[group]
            ).start()
        for which, (source, target) in enumerate(((q_hbm, q_buf), (g_hbm, g_buf))):
            pltpu.make_async_copy(
                source.at[0, :, cols(group, WIDTH)], target.at[group], load_sem.at[which, group]
            ).start()

    tables = [
        pltpu.make_async_copy(source, target, table_sem.at[slot])
        for slot, (source, target) in enumerate(
            ((end_hbm, end_ref), (list_hbm, list_ref), (count_hbm, count_ref))
        )
    ]
    for table in tables:
        table.start()
    load(0)

    def kv_copy(group, which, source, peer):
        return pltpu.make_async_remote_copy(
            src_ref=(k_hbm, v_hbm)[which].at[0, :, cols(group)],
            dst_ref=kv_buf.at[group, which, block(source)],
            send_sem=kv_send.at[peer, group, which],
            recv_sem=kv_recv.at[source, group],
            device_id={"ctx": peer},
            device_id_type=MESH,
        )

    def share_copy(group, source, peer):
        return pltpu.make_async_remote_copy(
            src_ref=share.at[group, :, pl.ds(peer * rows, rows)],
            dst_ref=shares_in.at[group, source],
            send_sem=share_send.at[peer, group],
            recv_sem=share_recv.at[source, group],
            device_id={"ctx": peer},
            device_id_type=MESH,
        )

    def query_copy(group, pair):
        return pltpu.make_async_remote_copy(
            src_ref=dq_buf.at[group, :, cols(pair, PAIR * HEAD_DIM)],
            dst_ref=out_q.at[0, :, cols(group * (RATIO // PAIR) + pair, PAIR * HEAD_DIM)],
            send_sem=dq_send.at[group],
            recv_sem=out_recv.at[0],
            device_id={"section": before},
            device_id_type=MESH,
        )

    def final_copy(group, which):
        return pltpu.make_async_remote_copy(
            src_ref=final.at[group, which],
            dst_ref=(out_k, out_v)[which].at[0, :, cols(group)],
            send_sem=final_send.at[which, group],
            recv_sem=out_recv.at[1 + which],
            device_id={"section": before},
            device_id_type=MESH,
        )

    def fill_bias(key_blocks):
        for low in range(blocks_here):
            query_block = ctx * blocks_here + low
            position = query_block * BLK + lax.broadcasted_iota(jnp.int32, (BLK, BLK), 0)
            for key_block in range(key_blocks):
                listed = jnp.int32(0)
                for entry in range(block_total):
                    hit = (list_ref[0, query_block, entry] == key_block) & (
                        entry < count_ref[0, query_block]
                    )
                    listed = listed | hit.astype(jnp.int32)
                key_place = key_block * BLK + lax.broadcasted_iota(jnp.int32, (BLK, BLK), 1)
                end = end_ref[:, key_block * BLK : (key_block + 1) * BLK] * listed
                allowed = (key_place <= position) & (position < end)
                bias[
                    key_block * BLK : (key_block + 1) * BLK, low * BLK : (low + 1) * BLK
                ] = jnp.where(allowed, 0.0, -jnp.inf).astype(F32).T

    def run(mine):
        length = (mine + 1) * rows
        for table in tables:
            table.wait()
        fill_bias((mine + 1) * blocks_here)
        pl.loop(1, KV_HEADS)(load)

        def send_keys(group):
            for peer in range(mine + 1, ctx_total):
                for which in range(2):
                    kv_copy(group, which, mine, peer).start()

        def enter():
            pl.semaphore_wait(barrier, 1 + ctx_total)
            if mine < ctx_total - 1:
                pl.when(section % 2 == 0)(lambda: send_keys(0))

        late = mine == ctx_total - 1
        if not late:
            enter()
        span = PAIR * rows

        def per_group(group, carry):
            if mine < ctx_total - 1:
                pl.when((section % 2 == 0) & (group + 1 < KV_HEADS))(lambda: send_keys(group + 1))
                pl.when(section % 2 == 1)(lambda: send_keys(group))
            for source in range(mine):
                pltpu.make_async_copy(
                    kv_buf.at[group, :, pl.ds(source * rows, rows)],
                    kv_buf.at[group, :, pl.ds(source * rows, rows)],
                    kv_recv.at[source, group],
                ).wait()
            pltpu.make_async_copy(
                kv_buf.at[group, :, pl.ds(mine * rows, rows)],
                kv_buf.at[group, :, pl.ds(mine * rows, rows)],
                kv_sem.at[group],
            ).wait()
            pltpu.make_async_copy(q_buf.at[group], q_buf.at[group], load_sem.at[0, group]).wait()
            pltpu.make_async_copy(g_buf.at[group], g_buf.at[group], load_sem.at[1, group]).wait()
            keys = kv_buf[group, 0, 0:length, :]
            values = kv_buf[group, 1, 0:length, :]

            def stacked(ref, first, count):
                parts = [ref[group, :, cols(first + low)] for low in range(count)]
                return jnp.concatenate(parts, axis=0)

            def per_pair(pair):
                here = slice(pair * span, pair * span + span)
                scores = contract(keys, stacked(q_buf, pair * PAIR, PAIR), 1, 1)
                masked = bias[0:length, :]
                scores = scores + jnp.concatenate([masked] * PAIR, axis=1)
                exponent = jnp.exp2((scores - jnp.max(scores, axis=0, keepdims=True)) * (scale * math.log2(math.e)))
                total = jnp.sum(exponent, axis=0, keepdims=True)
                attention = exponent * (1.0 / total)
                at_buf[0:length, here] = attention.astype(BF16)
                weight_grad = contract(values, stacked(g_buf, pair * PAIR, PAIR), 1, 1)
                row_delta = jnp.sum(attention * weight_grad, axis=0, keepdims=True)
                score_grad = (attention * (weight_grad - row_delta)).astype(BF16)
                ds_buf[0:length, here] = score_grad
                query_grad = (contract(score_grad, keys, 0, 0) * scale).astype(BF16)
                for low in range(PAIR):
                    dq_buf[group, :, cols(pair * PAIR + low)] = query_grad[low * rows : (low + 1) * rows]
                if late and pair == 0:
                    pl.when(group == 0)(enter)
                query_copy(group, pair).start()

            for pair in range(RATIO // PAIR):
                per_pair(pair)
            key_grad = contract(ds_buf[0:length, :], stacked(q_buf, 0, RATIO), 1, 0) * scale
            value_grad = contract(at_buf[0:length, :], stacked(g_buf, 0, RATIO), 1, 0)
            first = mine * rows
            if mine > 0:
                share[group, 0, 0:first, :] = key_grad[0:first].astype(BF16)
                share[group, 1, 0:first, :] = value_grad[0:first].astype(BF16)
                for peer in range(mine):
                    share_copy(group, mine, peer).start()
            if mine == ctx_total - 1:
                final[group, 0] = key_grad[first:].astype(BF16)
                final[group, 1] = value_grad[first:].astype(BF16)
                for which in range(2):
                    final_copy(group, which).start()
            else:
                own[group, 0] = key_grad[first:]
                own[group, 1] = value_grad[first:]
            return carry

        lax.fori_loop(0, KV_HEADS, per_group, 0)

        if mine < ctx_total - 1:

            @pl.loop(0, KV_HEADS)
            def _(group):
                total = own[group]
                for source in range(mine + 1, ctx_total):
                    share_copy(group, source, mine).wait_recv()
                    total = total + shares_in[group, source].astype(F32)
                final[group] = total.astype(BF16)
                for which in range(2):
                    final_copy(group, which).start()

        @pl.loop(0, KV_HEADS)
        def _(group):
            for peer in range(mine + 1, ctx_total):
                for which in range(2):
                    kv_copy(group, which, mine, peer).wait_send()
            for peer in range(mine):
                share_copy(group, mine, peer).wait_send()

    for mine in range(ctx_total):
        pl.when(ctx == mine)(functools.partial(run, mine))

    @pl.loop(0, KV_HEADS)
    def _(group):
        pltpu.make_async_copy(dq_buf.at[group], dq_buf.at[group], dq_send.at[group]).wait()
        for which in range(2):
            final_copy(group, which).wait_send()

    for slot, out in enumerate((out_q, out_k, out_v)):
        pltpu.make_async_copy(out, out, out_recv.at[slot]).wait()


def write_out(held_q, held_k, held_v, out_q, out_k, out_v, done):
    pairs = ((held_q, out_q), (held_k, out_k), (held_v, out_v))
    copies = [pltpu.make_async_copy(a, b, done.at[slot]) for slot, (a, b) in enumerate(pairs)]
    for copy in copies:
        copy.start()
    for copy in copies:
        copy.wait()


def per_device(
    section_total,
    ctx_total,
    queries,
    key_states,
    value_states,
    out_grad,
    node_end,
    block_list,
    block_count,
):
    rows = queries.shape[1]
    length = node_end.shape[1]
    anywhere = pl.BlockSpec(memory_space=pl.ANY)
    vector = pl.BlockSpec(memory_space=pltpu.VMEM)
    dma = pltpu.SemaphoreType.DMA
    tall = RATIO * rows
    held = pl.pallas_call(
        functools.partial(kernel, section_total, ctx_total),
        out_shape=(
            pltpu.VMEM(queries.shape, BF16),
            pltpu.VMEM(key_states.shape, BF16),
            pltpu.VMEM(value_states.shape, BF16),
        ),
        in_specs=[anywhere] * 7,
        out_specs=[vector] * 3,
        scratch_shapes=[
            pltpu.VMEM((KV_HEADS, rows, WIDTH), BF16),
            pltpu.VMEM((KV_HEADS, rows, WIDTH), BF16),
            pltpu.VMEM((KV_HEADS, 2, length, HEAD_DIM), BF16),
            pltpu.VMEM((KV_HEADS, rows, WIDTH), BF16),
            pltpu.VMEM((length, tall), BF16),
            pltpu.VMEM((length, tall), BF16),
            pltpu.VMEM((length, rows), F32),
            pltpu.VMEM((KV_HEADS, 2, rows, HEAD_DIM), F32),
            pltpu.VMEM((KV_HEADS, 2, length, HEAD_DIM), BF16),
            pltpu.VMEM((KV_HEADS, ctx_total, 2, rows, HEAD_DIM), BF16),
            pltpu.VMEM((KV_HEADS, 2, rows, HEAD_DIM), BF16),
            pltpu.VMEM(node_end.shape, jnp.int32),
            pltpu.SMEM(block_list.shape, jnp.int32),
            pltpu.SMEM(block_count.shape, jnp.int32),
            dma((3,)),
            dma((2, KV_HEADS)),
            dma((KV_HEADS,)),
            dma((ctx_total, KV_HEADS, 2)),
            dma((ctx_total, KV_HEADS)),
            dma((KV_HEADS,)),
            dma((ctx_total, KV_HEADS)),
            dma((ctx_total, KV_HEADS)),
            dma((2, KV_HEADS)),
            dma((3,)),
        ],
        compiler_params=pltpu.CompilerParams(collective_id=0, has_side_effects=True),
    )(queries, key_states, value_states, out_grad, node_end, block_list, block_count)
    return pl.pallas_call(
        write_out,
        out_shape=tuple(jax.ShapeDtypeStruct(part.shape, BF16) for part in held),
        in_specs=[anywhere] * 3,
        out_specs=[anywhere] * 3,
        scratch_shapes=[dma((len(held),))],
        compiler_params=pltpu.CompilerParams(vmem_limit_bytes=1 << 20),
    )(*held)


def solution(mesh):
    wide = P("section", "ctx", None)
    return jax.shard_map(
        functools.partial(per_device, mesh.shape["section"], mesh.shape["ctx"]),
        mesh=mesh,
        in_specs=(wide, wide, wide, wide, P("section", None), P("section", None, None), P("section", None)),
        out_specs=(wide, wide, wide),
        check_vma=False,
    )
```

```python
import functools
import math

import jax
import jax.numpy as jnp
from jax import lax
from jax.experimental import pallas as pl
from jax.experimental.pallas import tpu as pltpu
from jax.sharding import PartitionSpec as P

HEADS = 64
KV_HEADS = 8
HEAD_DIM = 128
BLK = 128
RATIO = HEADS // KV_HEADS
PAIR = 4
WIDTH = RATIO * HEAD_DIM
FOLDS = RATIO // 2
DIAG = 16

F32 = jnp.float32
BF16 = jnp.bfloat16
MESH = pl.DeviceIdType.MESH


def contract(left, right, left_dim, right_dim):
    return lax.dot_general(
        left, right, (((left_dim,), (right_dim,)), ((), ())), preferred_element_type=F32
    )


def kernel(
    section_total,
    ctx_total,
    q_hbm,
    k_hbm,
    v_hbm,
    g_hbm,
    end_hbm,
    list_hbm,
    count_hbm,
    out_q,
    out_k,
    out_v,
    q_buf,
    g_buf,
    kv_buf,
    dq_buf,
    ds_buf,
    at_buf,
    bias,
    own,
    share,
    shares_in,
    final,
    fold_out,
    fold_in,
    next_keys,
    relay,
    end_ref,
    list_ref,
    count_ref,
    table_sem,
    load_sem,
    kv_sem,
    kv_send,
    kv_recv,
    dq_send,
    share_send,
    share_recv,
    final_send,
    out_recv,
    fold_send,
    fold_recv,
    next_sem,
    relay_send,
    relay_recv,
):
    rows = q_hbm.shape[1]
    block_total = list_hbm.shape[1]
    blocks_here = rows // BLK
    scale = 1.0 / math.sqrt(HEAD_DIM)
    last = ctx_total - 1
    section = lax.axis_index("section")
    ctx = lax.axis_index("ctx")
    before = lax.rem(section + section_total - 1, section_total)
    after = lax.rem(section + 1, section_total)

    def cols(index, width=HEAD_DIM):
        if isinstance(index, int):
            return slice(index * width, index * width + width)
        return pl.ds(pl.multiple_of(index * width, width), width)

    def block(index):
        return pl.ds(pl.multiple_of(index * rows, rows), rows)

    barrier = pltpu.get_barrier_semaphore()
    for target in (before, after):
        pl.semaphore_signal(barrier, 1, device_id={"section": target}, device_id_type=MESH)
    for step in range(1, ctx_total):
        other = lax.rem(ctx + step, ctx_total)
        pl.semaphore_signal(barrier, 1, device_id={"ctx": other}, device_id_type=MESH)
    if last > 0:

        @pl.when(ctx == 0)
        def _():
            pl.semaphore_signal(
                barrier, 1, device_id={"section": after, "ctx": last}, device_id_type=MESH
            )

    def load(group):
        for which, source in enumerate((k_hbm, v_hbm)):
            pltpu.make_async_copy(
                source.at[0, :, cols(group)], kv_buf.at[group, which, block(ctx)], kv_sem.at[group]
            ).start()
        for which, (source, target) in enumerate(((q_hbm, q_buf), (g_hbm, g_buf))):
            pltpu.make_async_copy(
                source.at[0, :, cols(group, WIDTH)], target.at[group], load_sem.at[which, group]
            ).start()

    tables = [
        pltpu.make_async_copy(source, target, table_sem.at[slot])
        for slot, (source, target) in enumerate(
            ((end_hbm, end_ref), (list_hbm, list_ref), (count_hbm, count_ref))
        )
    ]
    for table in tables:
        table.start()
    load(0)

    def kv_copy(group, which, source, peer):
        return pltpu.make_async_remote_copy(
            src_ref=(k_hbm, v_hbm)[which].at[0, :, cols(group)],
            dst_ref=kv_buf.at[group, which, block(source)],
            send_sem=kv_send.at[peer, group, which],
            recv_sem=kv_recv.at[source, group],
            device_id={"ctx": peer},
            device_id_type=MESH,
        )

    def share_copy(group, source, peer):
        return pltpu.make_async_remote_copy(
            src_ref=share.at[group, :, pl.ds(peer * rows, rows)],
            dst_ref=shares_in.at[group, source],
            send_sem=share_send.at[peer, group],
            recv_sem=share_recv.at[source, group],
            device_id={"ctx": peer},
            device_id_type=MESH,
        )

    def query_copy(group, pair):
        return pltpu.make_async_remote_copy(
            src_ref=dq_buf.at[group, :, cols(pair, PAIR * HEAD_DIM)],
            dst_ref=out_q.at[0, :, cols(group * (RATIO // PAIR) + pair, PAIR * HEAD_DIM)],
            send_sem=dq_send.at[group],
            recv_sem=out_recv.at[0],
            device_id={"section": before},
            device_id_type=MESH,
        )

    def fold_copy(group):
        return pltpu.make_async_remote_copy(
            src_ref=fold_out.at[group],
            dst_ref=fold_in.at[group],
            send_sem=fold_send.at[group],
            recv_sem=fold_recv.at[group],
            device_id={"section": before},
            device_id_type=MESH,
        )

    def next_copy():
        return pltpu.make_async_remote_copy(
            src_ref=k_hbm.at[0],
            dst_ref=next_keys,
            send_sem=next_sem.at[0],
            recv_sem=next_sem.at[1],
            device_id={"section": before},
            device_id_type=MESH,
        )

    def detour_copy(group, which):
        return pltpu.make_async_remote_copy(
            src_ref=final.at[group, which],
            dst_ref=relay.at[group, which],
            send_sem=final_send.at[which, group],
            recv_sem=relay_recv.at[which, group],
            device_id={"section": before, "ctx": 0},
            device_id_type=MESH,
        )

    def relay_copy(group, which):
        return pltpu.make_async_remote_copy(
            src_ref=relay.at[group, which],
            dst_ref=(out_k, out_v)[which].at[0, :, cols(group)],
            send_sem=relay_send.at[which, group],
            recv_sem=out_recv.at[1 + which],
            device_id={"ctx": last},
            device_id_type=MESH,
        )

    def final_copy(group, which):
        return pltpu.make_async_remote_copy(
            src_ref=final.at[group, which],
            dst_ref=(out_k, out_v)[which].at[0, :, cols(group)],
            send_sem=final_send.at[which, group],
            recv_sem=out_recv.at[1 + which],
            device_id={"section": before},
            device_id_type=MESH,
        )

    def fill_bias(key_blocks):
        for low in range(blocks_here):
            query_block = ctx * blocks_here + low
            position = query_block * BLK + lax.broadcasted_iota(jnp.int32, (BLK, BLK), 0)
            for key_block in range(key_blocks):
                listed = jnp.int32(0)
                for entry in range(block_total):
                    hit = (list_ref[0, query_block, entry] == key_block) & (
                        entry < count_ref[0, query_block]
                    )
                    listed = listed | hit.astype(jnp.int32)
                key_place = key_block * BLK + lax.broadcasted_iota(jnp.int32, (BLK, BLK), 1)
                end = end_ref[:, key_block * BLK : (key_block + 1) * BLK] * listed
                allowed = (key_place <= position) & (position < end)
                bias[
                    key_block * BLK : (key_block + 1) * BLK, low * BLK : (low + 1) * BLK
                ] = jnp.where(allowed, 0.0, -jnp.inf).astype(F32).T

    def corner():
        down = lax.broadcasted_iota(jnp.int32, (rows, rows), 0)
        across = lax.broadcasted_iota(jnp.int32, (rows, rows), 1)
        return down, across

    def fold(group, score_float):
        down, across = corner()
        place = lax.broadcasted_iota(jnp.int32, (DIAG, rows), 0)
        diagonals = jnp.zeros((DIAG, rows), F32)
        for pair in range(FOLDS):
            upper = score_float[:, 2 * pair * rows : (2 * pair + 1) * rows]
            other = score_float[:, (2 * pair + 1) * rows : (2 * pair + 2) * rows]
            square = jnp.where(down <= across, upper, other.T)
            fold_out[group, pair * rows : (pair + 1) * rows, :] = square.astype(BF16)
            diagonal = jnp.sum(jnp.where(down == across, other, 0.0), axis=0, keepdims=True)
            diagonals = jnp.where(place == pair, diagonal, diagonals)
        fold_out[group, FOLDS * rows :, :] = diagonals.astype(BF16)

    def unfold(group):
        down, across = corner()
        keys = next_keys[:, cols(group)]
        diagonals = fold_in[group, FOLDS * rows :, :].astype(F32)
        uppers, lowers = [], []
        for pair in range(FOLDS):
            square = fold_in[group, pair * rows : (pair + 1) * rows, :].astype(F32)
            diagonal = diagonals[pair : pair + 1, :]
            uppers.append(jnp.where(down <= across, square, 0.0).astype(BF16))
            rest = jnp.where(down == across, diagonal, 0.0)
            lowers.append(jnp.where(down > across, square, rest).astype(BF16))
        even = contract(jnp.concatenate(uppers, axis=1), keys, 0, 0).astype(BF16)
        odd = contract(jnp.concatenate(lowers, axis=0), keys, 1, 0).astype(BF16)
        for pair in range(FOLDS):
            here = slice(pair * rows, (pair + 1) * rows)
            out_q[0, :, cols(group * RATIO + 2 * pair)] = even[here]
            out_q[0, :, cols(group * RATIO + 2 * pair + 1)] = odd[here]

    def run(mine):
        length = (mine + 1) * rows
        for table in tables:
            table.wait()
        fill_bias((mine + 1) * blocks_here)
        pl.loop(1, KV_HEADS)(load)

        def send_keys(group):
            for peer in range(mine + 1, ctx_total):
                for which in range(2):
                    kv_copy(group, which, mine, peer).start()

        def enter():
            pl.semaphore_wait(barrier, 1 + ctx_total + (1 if 0 < mine == last else 0))
            if mine < last:
                pl.when(section % 2 == 0)(lambda: send_keys(0))
            if mine == 0:
                next_copy().start()

        late = 0 < mine == last
        if not late:
            enter()
        heads = RATIO if mine == 0 else PAIR
        span = heads * rows

        def per_group(group, carry):
            if mine < ctx_total - 1:
                pl.when((section % 2 == 0) & (group + 1 < KV_HEADS))(lambda: send_keys(group + 1))
                pl.when(section % 2 == 1)(lambda: send_keys(group))
            for source in range(mine):
                pltpu.make_async_copy(
                    kv_buf.at[group, :, pl.ds(source * rows, rows)],
                    kv_buf.at[group, :, pl.ds(source * rows, rows)],
                    kv_recv.at[source, group],
                ).wait()
            pltpu.make_async_copy(
                kv_buf.at[group, :, pl.ds(mine * rows, rows)],
                kv_buf.at[group, :, pl.ds(mine * rows, rows)],
                kv_sem.at[group],
            ).wait()
            pltpu.make_async_copy(q_buf.at[group], q_buf.at[group], load_sem.at[0, group]).wait()
            pltpu.make_async_copy(g_buf.at[group], g_buf.at[group], load_sem.at[1, group]).wait()
            keys = kv_buf[group, 0, 0:length, :]
            values = kv_buf[group, 1, 0:length, :]

            def stacked(ref, first, count):
                parts = [ref[group, :, cols(first + low)] for low in range(count)]
                return jnp.concatenate(parts, axis=0)

            def per_pair(pair):
                here = slice(pair * span, pair * span + span)
                scores = contract(keys, stacked(q_buf, pair * heads, heads), 1, 1)
                masked = bias[0:length, :]
                scores = scores + jnp.concatenate([masked] * heads, axis=1)
                shifted = scores - jnp.max(scores, axis=0, keepdims=True)
                exponent = jnp.exp2(shifted * (scale * math.log2(math.e)))
                total = jnp.sum(exponent, axis=0, keepdims=True)
                attention = exponent * (1.0 / total)
                at_buf[0:length, here] = attention.astype(BF16)
                weight_grad = contract(values, stacked(g_buf, pair * heads, heads), 1, 1)
                row_delta = jnp.sum(attention * weight_grad, axis=0, keepdims=True)
                score_float = attention * (weight_grad - row_delta) * scale
                score_grad = score_float.astype(BF16)
                ds_buf[0:length, here] = score_grad
                if mine == 0:
                    fold(group, score_float)
                    fold_copy(group).start()
                    return
                query_grad = contract(score_grad, keys, 0, 0).astype(BF16)
                for low in range(heads):
                    dq_buf[group, :, cols(pair * heads + low)] = query_grad[low * rows : (low + 1) * rows]
                if late and pair == 0:
                    pl.when(group == 0)(enter)
                query_copy(group, pair).start()

            for pair in range(RATIO // heads):
                per_pair(pair)
            key_grad = contract(ds_buf[0:length, :], stacked(q_buf, 0, RATIO), 1, 0)
            value_grad = contract(at_buf[0:length, :], stacked(g_buf, 0, RATIO), 1, 0)
            first = mine * rows
            if mine > 0:
                share[group, 0, 0:first, :] = key_grad[0:first].astype(BF16)
                share[group, 1, 0:first, :] = value_grad[0:first].astype(BF16)
                for peer in range(mine):
                    share_copy(group, mine, peer).start()
            if mine == ctx_total - 1:
                final[group, 0] = key_grad[first:].astype(BF16)
                final[group, 1] = value_grad[first:].astype(BF16)
                for which in range(2):
                    if mine > 0:
                        pl.when(section % 2 == 0)(detour_copy(group, which).start)
                        pl.when(section % 2 == 1)(final_copy(group, which).start)
                    else:
                        final_copy(group, which).start()
            else:
                own[group, 0] = key_grad[first:]
                own[group, 1] = value_grad[first:]
            return carry

        lax.fori_loop(0, KV_HEADS, per_group, 0)

        if mine == 0:
            next_copy().wait_recv()

        def finish(group):
            if mine == 0:
                fold_copy(group).wait_recv()
                unfold(group)
            if mine < last:
                total = own[group]
                for source in range(mine + 1, ctx_total):
                    share_copy(group, source, mine).wait_recv()
                    total = total + shares_in[group, source].astype(F32)
                final[group] = total.astype(BF16)
                for which in range(2):
                    final_copy(group, which).start()
            if mine == 0 and last > 0:

                @pl.when(after % 2 == 0)
                def _():
                    for which in range(2):
                        detour_copy(group, which).wait_recv()
                        relay_copy(group, which).start()

        if mine < last or mine == 0:
            pl.loop(0, KV_HEADS)(finish)

        @pl.loop(0, KV_HEADS)
        def _(group):
            for peer in range(mine + 1, ctx_total):
                for which in range(2):
                    kv_copy(group, which, mine, peer).wait_send()
            for peer in range(mine):
                share_copy(group, mine, peer).wait_send()
            for which in range(2):
                final_copy(group, which).wait_send()
            if mine > 0:
                pltpu.make_async_copy(dq_buf.at[group], dq_buf.at[group], dq_send.at[group]).wait()
            else:
                fold_copy(group).wait_send()
            if mine == 0 and last > 0:

                @pl.when(after % 2 == 0)
                def _():
                    for which in range(2):
                        relay_copy(group, which).wait_send()

        if mine == 0:
            next_copy().wait_send()
        else:
            pltpu.make_async_copy(out_q, out_q, out_recv.at[0]).wait()

    for mine in range(ctx_total):
        pl.when(ctx == mine)(functools.partial(run, mine))

    for slot, out in ((1, out_k), (2, out_v)):
        pltpu.make_async_copy(out, out, out_recv.at[slot]).wait()


def write_out(held_q, held_k, held_v, out_q, out_k, out_v, done):
    pairs = ((held_q, out_q), (held_k, out_k), (held_v, out_v))
    copies = [pltpu.make_async_copy(a, b, done.at[slot]) for slot, (a, b) in enumerate(pairs)]
    for copy in copies:
        copy.start()
    for copy in copies:
        copy.wait()


def per_device(
    section_total,
    ctx_total,
    queries,
    key_states,
    value_states,
    out_grad,
    node_end,
    block_list,
    block_count,
):
    rows = queries.shape[1]
    length = node_end.shape[1]
    anywhere = pl.BlockSpec(memory_space=pl.ANY)
    vector = pl.BlockSpec(memory_space=pltpu.VMEM)
    dma = pltpu.SemaphoreType.DMA
    tall = RATIO * rows
    held = pl.pallas_call(
        functools.partial(kernel, section_total, ctx_total),
        out_shape=(
            pltpu.VMEM(queries.shape, BF16),
            pltpu.VMEM(key_states.shape, BF16),
            pltpu.VMEM(value_states.shape, BF16),
        ),
        in_specs=[anywhere] * 7,
        out_specs=[vector] * 3,
        scratch_shapes=[
            pltpu.VMEM((KV_HEADS, rows, WIDTH), BF16),
            pltpu.VMEM((KV_HEADS, rows, WIDTH), BF16),
            pltpu.VMEM((KV_HEADS, 2, length, HEAD_DIM), BF16),
            pltpu.VMEM((KV_HEADS, rows, WIDTH), BF16),
            pltpu.VMEM((length, tall), BF16),
            pltpu.VMEM((length, tall), BF16),
            pltpu.VMEM((length, rows), F32),
            pltpu.VMEM((KV_HEADS, 2, rows, HEAD_DIM), F32),
            pltpu.VMEM((KV_HEADS, 2, length, HEAD_DIM), BF16),
            pltpu.VMEM((KV_HEADS, ctx_total, 2, rows, HEAD_DIM), BF16),
            pltpu.VMEM((KV_HEADS, 2, rows, HEAD_DIM), BF16),
            pltpu.VMEM((KV_HEADS, FOLDS * rows + DIAG, rows), BF16),
            pltpu.VMEM((KV_HEADS, FOLDS * rows + DIAG, rows), BF16),
            pltpu.VMEM((rows, KV_HEADS * HEAD_DIM), BF16),
            pltpu.VMEM((KV_HEADS, 2, rows, HEAD_DIM), BF16),
            pltpu.VMEM(node_end.shape, jnp.int32),
            pltpu.SMEM(block_list.shape, jnp.int32),
            pltpu.SMEM(block_count.shape, jnp.int32),
            dma((3,)),
            dma((2, KV_HEADS)),
            dma((KV_HEADS,)),
            dma((ctx_total, KV_HEADS, 2)),
            dma((ctx_total, KV_HEADS)),
            dma((KV_HEADS,)),
            dma((ctx_total, KV_HEADS)),
            dma((ctx_total, KV_HEADS)),
            dma((2, KV_HEADS)),
            dma((3,)),
            dma((KV_HEADS,)),
            dma((KV_HEADS,)),
            dma((2,)),
            dma((2, KV_HEADS)),
            dma((2, KV_HEADS)),
        ],
        compiler_params=pltpu.CompilerParams(collective_id=0, has_side_effects=True),
    )(queries, key_states, value_states, out_grad, node_end, block_list, block_count)
    return pl.pallas_call(
        write_out,
        out_shape=tuple(jax.ShapeDtypeStruct(part.shape, BF16) for part in held),
        in_specs=[anywhere] * 3,
        out_specs=[anywhere] * 3,
        scratch_shapes=[dma((len(held),))],
        compiler_params=pltpu.CompilerParams(vmem_limit_bytes=1 << 20),
    )(*held)


def solution(mesh):
    wide = P("section", "ctx", None)
    return jax.shard_map(
        functools.partial(per_device, mesh.shape["section"], mesh.shape["ctx"]),
        mesh=mesh,
        in_specs=(wide, wide, wide, wide, P("section", None), P("section", None, None), P("section", None)),
        out_specs=(wide, wide, wide),
        check_vma=False,
    )
```

```python
import functools
import math

import jax
import jax.numpy as jnp
from jax import lax
from jax.experimental import pallas as pl
from jax.experimental.pallas import tpu as pltpu
from jax.sharding import PartitionSpec as P

HEADS = 64
KV_HEADS = 8
HEAD_DIM = 128
BLK = 128
RATIO = HEADS // KV_HEADS
PAIR = 4
WIDTH = RATIO * HEAD_DIM
FOLDS = RATIO // 2
DIAG = 16

F32 = jnp.float32
BF16 = jnp.bfloat16
MESH = pl.DeviceIdType.MESH


def contract(left, right, left_dim, right_dim):
    return lax.dot_general(
        left, right, (((left_dim,), (right_dim,)), ((), ())), preferred_element_type=F32
    )


def kernel(
    section_total,
    ctx_total,
    q_hbm,
    k_hbm,
    v_hbm,
    g_hbm,
    end_hbm,
    list_hbm,
    count_hbm,
    out_q,
    out_k,
    out_v,
    q_buf,
    g_buf,
    kv_buf,
    dq_buf,
    ds_buf,
    at_buf,
    bias,
    own,
    share,
    shares_in,
    final,
    fold_out,
    fold_in,
    next_keys,
    aside,
    relay,
    end_ref,
    list_ref,
    count_ref,
    table_sem,
    load_sem,
    kv_sem,
    kv_send,
    kv_recv,
    dq_send,
    share_send,
    share_recv,
    final_send,
    out_recv,
    fold_send,
    fold_recv,
    next_sem,
    aside_send,
    aside_recv,
    relay_send,
    relay_recv,
):
    rows = q_hbm.shape[1]
    block_total = list_hbm.shape[1]
    blocks_here = rows // BLK
    scale = 1.0 / math.sqrt(HEAD_DIM)
    last = ctx_total - 1
    section = lax.axis_index("section")
    ctx = lax.axis_index("ctx")
    before = lax.rem(section + section_total - 1, section_total)
    after = lax.rem(section + 1, section_total)

    def cols(index, width=HEAD_DIM):
        if isinstance(index, int):
            return slice(index * width, index * width + width)
        return pl.ds(pl.multiple_of(index * width, width), width)

    def block(index):
        return pl.ds(pl.multiple_of(index * rows, rows), rows)

    barrier = pltpu.get_barrier_semaphore()
    for target in (before, after):
        pl.semaphore_signal(barrier, 1, device_id={"section": target}, device_id_type=MESH)
    for step in range(1, ctx_total):
        other = lax.rem(ctx + step, ctx_total)
        pl.semaphore_signal(barrier, 1, device_id={"ctx": other}, device_id_type=MESH)
    def load(group):
        for which, source in enumerate((k_hbm, v_hbm)):
            pltpu.make_async_copy(
                source.at[0, :, cols(group)], kv_buf.at[group, which, block(ctx)], kv_sem.at[group]
            ).start()
        for which, (source, target) in enumerate(((q_hbm, q_buf), (g_hbm, g_buf))):
            pltpu.make_async_copy(
                source.at[0, :, cols(group, WIDTH)], target.at[group], load_sem.at[which, group]
            ).start()

    tables = [
        pltpu.make_async_copy(source, target, table_sem.at[slot])
        for slot, (source, target) in enumerate(
            ((end_hbm, end_ref), (list_hbm, list_ref), (count_hbm, count_ref))
        )
    ]
    for table in tables:
        table.start()
    load(0)

    def kv_copy(group, which, source, peer):
        return pltpu.make_async_remote_copy(
            src_ref=(k_hbm, v_hbm)[which].at[0, :, cols(group)],
            dst_ref=kv_buf.at[group, which, block(source)],
            send_sem=kv_send.at[peer, group, which],
            recv_sem=kv_recv.at[source, group],
            device_id={"ctx": peer},
            device_id_type=MESH,
        )

    def share_copy(group, source, peer):
        return pltpu.make_async_remote_copy(
            src_ref=share.at[group, :, pl.ds(peer * rows, rows)],
            dst_ref=shares_in.at[group, source],
            send_sem=share_send.at[peer, group],
            recv_sem=share_recv.at[source, group],
            device_id={"ctx": peer},
            device_id_type=MESH,
        )

    def query_copy(group, pair):
        return pltpu.make_async_remote_copy(
            src_ref=dq_buf.at[group, :, cols(pair, PAIR * HEAD_DIM)],
            dst_ref=out_q.at[0, :, cols(group * (RATIO // PAIR) + pair, PAIR * HEAD_DIM)],
            send_sem=dq_send.at[group],
            recv_sem=out_recv.at[0],
            device_id={"section": before},
            device_id_type=MESH,
        )

    def fold_copy(group):
        return pltpu.make_async_remote_copy(
            src_ref=fold_out.at[group],
            dst_ref=fold_in.at[group],
            send_sem=fold_send.at[group],
            recv_sem=fold_recv.at[group],
            device_id={"section": before},
            device_id_type=MESH,
        )

    def next_copy():
        return pltpu.make_async_remote_copy(
            src_ref=k_hbm.at[0],
            dst_ref=next_keys,
            send_sem=next_sem.at[0],
            recv_sem=next_sem.at[1],
            device_id={"section": before},
            device_id_type=MESH,
        )

    def aside_copy(group, which):
        return pltpu.make_async_remote_copy(
            src_ref=final.at[group, which],
            dst_ref=aside.at[group, which],
            send_sem=final_send.at[which, group],
            recv_sem=aside_recv.at[which, group],
            device_id={"ctx": 0},
            device_id_type=MESH,
        )

    def detour_copy(group, which):
        return pltpu.make_async_remote_copy(
            src_ref=aside.at[group, which],
            dst_ref=relay.at[group, which],
            send_sem=aside_send.at[which, group],
            recv_sem=relay_recv.at[which, group],
            device_id={"section": before},
            device_id_type=MESH,
        )

    def relay_copy(group, which):
        return pltpu.make_async_remote_copy(
            src_ref=relay.at[group, which],
            dst_ref=(out_k, out_v)[which].at[0, :, cols(group)],
            send_sem=relay_send.at[which, group],
            recv_sem=out_recv.at[1 + which],
            device_id={"ctx": last},
            device_id_type=MESH,
        )

    def final_copy(group, which):
        return pltpu.make_async_remote_copy(
            src_ref=final.at[group, which],
            dst_ref=(out_k, out_v)[which].at[0, :, cols(group)],
            send_sem=final_send.at[which, group],
            recv_sem=out_recv.at[1 + which],
            device_id={"section": before},
            device_id_type=MESH,
        )

    def fill_bias(key_blocks):
        for low in range(blocks_here):
            query_block = ctx * blocks_here + low
            position = query_block * BLK + lax.broadcasted_iota(jnp.int32, (BLK, BLK), 0)
            for key_block in range(key_blocks):
                listed = jnp.int32(0)
                for entry in range(block_total):
                    hit = (list_ref[0, query_block, entry] == key_block) & (
                        entry < count_ref[0, query_block]
                    )
                    listed = listed | hit.astype(jnp.int32)
                key_place = key_block * BLK + lax.broadcasted_iota(jnp.int32, (BLK, BLK), 1)
                end = end_ref[:, key_block * BLK : (key_block + 1) * BLK] * listed
                allowed = (key_place <= position) & (position < end)
                bias[
                    key_block * BLK : (key_block + 1) * BLK, low * BLK : (low + 1) * BLK
                ] = jnp.where(allowed, 0.0, -jnp.inf).astype(F32).T

    def corner():
        down = lax.broadcasted_iota(jnp.int32, (rows, rows), 0)
        across = lax.broadcasted_iota(jnp.int32, (rows, rows), 1)
        return down, across

    def fold(group, score_float):
        down, across = corner()
        place = lax.broadcasted_iota(jnp.int32, (DIAG, rows), 0)
        diagonals = jnp.zeros((DIAG, rows), F32)
        for pair in range(FOLDS):
            upper = score_float[:, 2 * pair * rows : (2 * pair + 1) * rows]
            other = score_float[:, (2 * pair + 1) * rows : (2 * pair + 2) * rows]
            square = jnp.where(down <= across, upper, other.T)
            fold_out[group, pair * rows : (pair + 1) * rows, :] = square.astype(BF16)
            diagonal = jnp.sum(jnp.where(down == across, other, 0.0), axis=0, keepdims=True)
            diagonals = jnp.where(place == pair, diagonal, diagonals)
        fold_out[group, FOLDS * rows :, :] = diagonals.astype(BF16)

    def unfold(group):
        down, across = corner()
        keys = next_keys[:, cols(group)]
        diagonals = fold_in[group, FOLDS * rows :, :].astype(F32)
        uppers, lowers = [], []
        for pair in range(FOLDS):
            square = fold_in[group, pair * rows : (pair + 1) * rows, :].astype(F32)
            diagonal = diagonals[pair : pair + 1, :]
            uppers.append(jnp.where(down <= across, square, 0.0).astype(BF16))
            rest = jnp.where(down == across, diagonal, 0.0)
            lowers.append(jnp.where(down > across, square, rest).astype(BF16))
        even = contract(jnp.concatenate(uppers, axis=1), keys, 0, 0).astype(BF16)
        odd = contract(jnp.concatenate(lowers, axis=0), keys, 1, 0).astype(BF16)
        for pair in range(FOLDS):
            here = slice(pair * rows, (pair + 1) * rows)
            out_q[0, :, cols(group * RATIO + 2 * pair)] = even[here]
            out_q[0, :, cols(group * RATIO + 2 * pair + 1)] = odd[here]

    def run(mine):
        length = (mine + 1) * rows
        for table in tables:
            table.wait()
        fill_bias((mine + 1) * blocks_here)
        pl.loop(1, KV_HEADS)(load)

        def send_keys(group):
            for peer in range(mine + 1, ctx_total):
                for which in range(2):
                    kv_copy(group, which, mine, peer).start()

        def enter():
            pl.semaphore_wait(barrier, 1 + ctx_total)
            if mine < last:
                pl.when(section % 2 == 0)(lambda: send_keys(0))
            if mine == 0:
                next_copy().start()

        late = 0 < mine == last
        if not late:
            enter()
        heads = RATIO if mine == 0 else PAIR
        span = heads * rows

        def per_group(group, carry):
            if mine < ctx_total - 1:
                pl.when((section % 2 == 0) & (group + 1 < KV_HEADS))(lambda: send_keys(group + 1))
                pl.when(section % 2 == 1)(lambda: send_keys(group))
            for source in range(mine):
                pltpu.make_async_copy(
                    kv_buf.at[group, :, pl.ds(source * rows, rows)],
                    kv_buf.at[group, :, pl.ds(source * rows, rows)],
                    kv_recv.at[source, group],
                ).wait()
            pltpu.make_async_copy(
                kv_buf.at[group, :, pl.ds(mine * rows, rows)],
                kv_buf.at[group, :, pl.ds(mine * rows, rows)],
                kv_sem.at[group],
            ).wait()
            pltpu.make_async_copy(q_buf.at[group], q_buf.at[group], load_sem.at[0, group]).wait()
            pltpu.make_async_copy(g_buf.at[group], g_buf.at[group], load_sem.at[1, group]).wait()
            keys = kv_buf[group, 0, 0:length, :]
            values = kv_buf[group, 1, 0:length, :]

            def stacked(ref, first, count):
                parts = [ref[group, :, cols(first + low)] for low in range(count)]
                return jnp.concatenate(parts, axis=0)

            def per_pair(pair):
                here = slice(pair * span, pair * span + span)
                scores = contract(keys, stacked(q_buf, pair * heads, heads), 1, 1)
                masked = bias[0:length, :]
                scores = scores + jnp.concatenate([masked] * heads, axis=1)
                shifted = scores - jnp.max(scores, axis=0, keepdims=True)
                exponent = jnp.exp2(shifted * (scale * math.log2(math.e)))
                total = jnp.sum(exponent, axis=0, keepdims=True)
                attention = exponent * (1.0 / total)
                at_buf[0:length, here] = attention.astype(BF16)
                weight_grad = contract(values, stacked(g_buf, pair * heads, heads), 1, 1)
                row_delta = jnp.sum(attention * weight_grad, axis=0, keepdims=True)
                score_float = attention * (weight_grad - row_delta) * scale
                score_grad = score_float.astype(BF16)
                ds_buf[0:length, here] = score_grad
                if mine == 0:
                    fold(group, score_float)
                    fold_copy(group).start()
                    return
                query_grad = contract(score_grad, keys, 0, 0).astype(BF16)
                for low in range(heads):
                    dq_buf[group, :, cols(pair * heads + low)] = query_grad[low * rows : (low + 1) * rows]
                if late and pair == 0:
                    pl.when(group == 0)(enter)
                query_copy(group, pair).start()

            for pair in range(RATIO // heads):
                per_pair(pair)
            key_grad = contract(ds_buf[0:length, :], stacked(q_buf, 0, RATIO), 1, 0)
            value_grad = contract(at_buf[0:length, :], stacked(g_buf, 0, RATIO), 1, 0)
            first = mine * rows
            if mine > 0:
                share[group, 0, 0:first, :] = key_grad[0:first].astype(BF16)
                share[group, 1, 0:first, :] = value_grad[0:first].astype(BF16)
                for peer in range(mine):
                    share_copy(group, mine, peer).start()
            if mine == ctx_total - 1:
                final[group, 0] = key_grad[first:].astype(BF16)
                final[group, 1] = value_grad[first:].astype(BF16)
                for which in range(2):
                    if mine > 0:
                        pl.when(section % 2 == 0)(aside_copy(group, which).start)
                        pl.when(section % 2 == 1)(final_copy(group, which).start)
                    else:
                        final_copy(group, which).start()
            else:
                own[group, 0] = key_grad[first:]
                own[group, 1] = value_grad[first:]
            return carry

        lax.fori_loop(0, KV_HEADS, per_group, 0)

        if mine == 0:
            next_copy().wait_recv()

        def forward(group):
            for which in range(2):
                aside_copy(group, which).wait_recv()
                detour_copy(group, which).start()

        def hand_over(group):
            for which in range(2):
                detour_copy(group, which).wait_recv()
                relay_copy(group, which).start()

        def finish(group):
            if mine == 0:
                fold_copy(group).wait_recv()
                unfold(group)
            if mine < last:
                total = own[group]
                for source in range(mine + 1, ctx_total):
                    share_copy(group, source, mine).wait_recv()
                    total = total + shares_in[group, source].astype(F32)
                final[group] = total.astype(BF16)
                for which in range(2):
                    final_copy(group, which).start()
            if mine == 0 and last > 0:
                pl.when(section % 2 == 0)(lambda: forward(group))
                pl.when((after % 2 == 0) & (group > 0))(lambda: hand_over(group - 1))

        if mine < last or mine == 0:
            pl.loop(0, KV_HEADS)(finish)
        if mine == 0 and last > 0:
            pl.when(after % 2 == 0)(lambda: hand_over(KV_HEADS - 1))

        @pl.loop(0, KV_HEADS)
        def _(group):
            for peer in range(mine + 1, ctx_total):
                for which in range(2):
                    kv_copy(group, which, mine, peer).wait_send()
            for peer in range(mine):
                share_copy(group, mine, peer).wait_send()
            for which in range(2):
                final_copy(group, which).wait_send()
            if mine > 0:
                pltpu.make_async_copy(dq_buf.at[group], dq_buf.at[group], dq_send.at[group]).wait()
            else:
                fold_copy(group).wait_send()
            if mine == 0 and last > 0:

                @pl.when(after % 2 == 0)
                def _():
                    for which in range(2):
                        relay_copy(group, which).wait_send()

                @pl.when(section % 2 == 0)
                def _():
                    for which in range(2):
                        detour_copy(group, which).wait_send()

        if mine == 0:
            next_copy().wait_send()
        else:
            pltpu.make_async_copy(out_q, out_q, out_recv.at[0]).wait()

    for mine in range(ctx_total):
        pl.when(ctx == mine)(functools.partial(run, mine))

    for slot, out in ((1, out_k), (2, out_v)):
        pltpu.make_async_copy(out, out, out_recv.at[slot]).wait()


def write_out(held_q, held_k, held_v, out_q, out_k, out_v, done):
    pairs = ((held_q, out_q), (held_k, out_k), (held_v, out_v))
    copies = [pltpu.make_async_copy(a, b, done.at[slot]) for slot, (a, b) in enumerate(pairs)]
    for copy in copies:
        copy.start()
    for copy in copies:
        copy.wait()


def per_device(
    section_total,
    ctx_total,
    queries,
    key_states,
    value_states,
    out_grad,
    node_end,
    block_list,
    block_count,
):
    rows = queries.shape[1]
    length = node_end.shape[1]
    anywhere = pl.BlockSpec(memory_space=pl.ANY)
    vector = pl.BlockSpec(memory_space=pltpu.VMEM)
    dma = pltpu.SemaphoreType.DMA
    tall = RATIO * rows
    held = pl.pallas_call(
        functools.partial(kernel, section_total, ctx_total),
        out_shape=(
            pltpu.VMEM(queries.shape, BF16),
            pltpu.VMEM(key_states.shape, BF16),
            pltpu.VMEM(value_states.shape, BF16),
        ),
        in_specs=[anywhere] * 7,
        out_specs=[vector] * 3,
        scratch_shapes=[
            pltpu.VMEM((KV_HEADS, rows, WIDTH), BF16),
            pltpu.VMEM((KV_HEADS, rows, WIDTH), BF16),
            pltpu.VMEM((KV_HEADS, 2, length, HEAD_DIM), BF16),
            pltpu.VMEM((KV_HEADS, rows, WIDTH), BF16),
            pltpu.VMEM((length, tall), BF16),
            pltpu.VMEM((length, tall), BF16),
            pltpu.VMEM((length, rows), F32),
            pltpu.VMEM((KV_HEADS, 2, rows, HEAD_DIM), F32),
            pltpu.VMEM((KV_HEADS, 2, length, HEAD_DIM), BF16),
            pltpu.VMEM((KV_HEADS, ctx_total, 2, rows, HEAD_DIM), BF16),
            pltpu.VMEM((KV_HEADS, 2, rows, HEAD_DIM), BF16),
            pltpu.VMEM((KV_HEADS, FOLDS * rows + DIAG, rows), BF16),
            pltpu.VMEM((KV_HEADS, FOLDS * rows + DIAG, rows), BF16),
            pltpu.VMEM((rows, KV_HEADS * HEAD_DIM), BF16),
            pltpu.VMEM((KV_HEADS, 2, rows, HEAD_DIM), BF16),
            pltpu.VMEM((KV_HEADS, 2, rows, HEAD_DIM), BF16),
            pltpu.VMEM(node_end.shape, jnp.int32),
            pltpu.SMEM(block_list.shape, jnp.int32),
            pltpu.SMEM(block_count.shape, jnp.int32),
            dma((3,)),
            dma((2, KV_HEADS)),
            dma((KV_HEADS,)),
            dma((ctx_total, KV_HEADS, 2)),
            dma((ctx_total, KV_HEADS)),
            dma((KV_HEADS,)),
            dma((ctx_total, KV_HEADS)),
            dma((ctx_total, KV_HEADS)),
            dma((2, KV_HEADS)),
            dma((3,)),
            dma((KV_HEADS,)),
            dma((KV_HEADS,)),
            dma((2,)),
            dma((2, KV_HEADS)),
            dma((2, KV_HEADS)),
            dma((2, KV_HEADS)),
            dma((2, KV_HEADS)),
        ],
        compiler_params=pltpu.CompilerParams(collective_id=0, has_side_effects=True),
    )(queries, key_states, value_states, out_grad, node_end, block_list, block_count)
    return pl.pallas_call(
        write_out,
        out_shape=tuple(jax.ShapeDtypeStruct(part.shape, BF16) for part in held),
        in_specs=[anywhere] * 3,
        out_specs=[anywhere] * 3,
        scratch_shapes=[dma((len(held),))],
        compiler_params=pltpu.CompilerParams(vmem_limit_bytes=1 << 20),
    )(*held)


def solution(mesh):
    wide = P("section", "ctx", None)
    return jax.shard_map(
        functools.partial(per_device, mesh.shape["section"], mesh.shape["ctx"]),
        mesh=mesh,
        in_specs=(wide, wide, wide, wide, P("section", None), P("section", None, None), P("section", None)),
        out_specs=(wide, wide, wide),
        check_vma=False,
    )
```

```python
import functools
import math

import jax
import jax.numpy as jnp
from jax import lax
from jax.experimental import pallas as pl
from jax.experimental.pallas import tpu as pltpu
from jax.sharding import PartitionSpec as P

HEADS = 64
KV_HEADS = 8
HEAD_DIM = 128
BLK = 128
RATIO = HEADS // KV_HEADS
PAIR = 4
WIDTH = RATIO * HEAD_DIM
FOLDS = RATIO // 2
DIAG = 16
DIRECT = 1
DIRECT_WRAP = 2

F32 = jnp.float32
BF16 = jnp.bfloat16
MESH = pl.DeviceIdType.MESH


def contract(left, right, left_dim, right_dim):
    return lax.dot_general(
        left, right, (((left_dim,), (right_dim,)), ((), ())), preferred_element_type=F32
    )


def kernel(
    section_total,
    ctx_total,
    q_hbm,
    k_hbm,
    v_hbm,
    g_hbm,
    end_hbm,
    list_hbm,
    count_hbm,
    out_q,
    out_k,
    out_v,
    q_buf,
    g_buf,
    kv_buf,
    dq_buf,
    ds_buf,
    at_buf,
    bias,
    own,
    share,
    shares_in,
    final,
    fold_out,
    fold_in,
    next_keys,
    aside,
    relay,
    end_ref,
    list_ref,
    count_ref,
    table_sem,
    load_sem,
    kv_sem,
    kv_send,
    kv_recv,
    dq_send,
    share_send,
    share_recv,
    final_send,
    out_recv,
    fold_send,
    fold_recv,
    next_sem,
    aside_send,
    aside_recv,
    relay_send,
    relay_recv,
    ready,
):
    rows = q_hbm.shape[1]
    block_total = list_hbm.shape[1]
    blocks_here = rows // BLK
    scale = 1.0 / math.sqrt(HEAD_DIM)
    last = ctx_total - 1
    section = lax.axis_index("section")
    ctx = lax.axis_index("ctx")
    before = lax.rem(section + section_total - 1, section_total)
    after = lax.rem(section + 1, section_total)

    def detoured(source, group):
        direct = jnp.where(source == 0, DIRECT_WRAP, DIRECT)
        return (source % 2 == 0) & (group < KV_HEADS - direct)

    def cols(index, width=HEAD_DIM):
        if isinstance(index, int):
            return slice(index * width, index * width + width)
        return pl.ds(pl.multiple_of(index * width, width), width)

    def block(index):
        return pl.ds(pl.multiple_of(index * rows, rows), rows)

    barrier = pltpu.get_barrier_semaphore()

    @pl.when(section % 2 == 0)
    def _():
        for target in (before, after):
            pl.semaphore_signal(barrier, 1, device_id={"section": target}, device_id_type=MESH)

    for step in range(1, ctx_total):
        other = lax.rem(ctx + step, ctx_total)
        pl.semaphore_signal(barrier, 1, device_id={"ctx": other}, device_id_type=MESH)
    def load(group):
        for which, source in enumerate((k_hbm, v_hbm)):
            pltpu.make_async_copy(
                source.at[0, :, cols(group)], kv_buf.at[group, which, block(ctx)], kv_sem.at[group]
            ).start()
        for which, (source, target) in enumerate(((q_hbm, q_buf), (g_hbm, g_buf))):
            pltpu.make_async_copy(
                source.at[0, :, cols(group, WIDTH)], target.at[group], load_sem.at[which, group]
            ).start()

    tables = [
        pltpu.make_async_copy(source, target, table_sem.at[slot])
        for slot, (source, target) in enumerate(
            ((end_hbm, end_ref), (list_hbm, list_ref), (count_hbm, count_ref))
        )
    ]
    for table in tables:
        table.start()
    load(0)

    def kv_copy(group, which, source, peer):
        return pltpu.make_async_remote_copy(
            src_ref=(k_hbm, v_hbm)[which].at[0, :, cols(group)],
            dst_ref=kv_buf.at[group, which, block(source)],
            send_sem=kv_send.at[peer, group, which],
            recv_sem=kv_recv.at[source, group],
            device_id={"ctx": peer},
            device_id_type=MESH,
        )

    def share_copy(group, source, peer):
        return pltpu.make_async_remote_copy(
            src_ref=share.at[group, :, pl.ds(peer * rows, rows)],
            dst_ref=shares_in.at[group, source],
            send_sem=share_send.at[peer, group],
            recv_sem=share_recv.at[source, group],
            device_id={"ctx": peer},
            device_id_type=MESH,
        )

    def query_copy(group, pair):
        return pltpu.make_async_remote_copy(
            src_ref=dq_buf.at[group, :, cols(pair, PAIR * HEAD_DIM)],
            dst_ref=out_q.at[0, :, cols(group * (RATIO // PAIR) + pair, PAIR * HEAD_DIM)],
            send_sem=dq_send.at[group],
            recv_sem=out_recv.at[0],
            device_id={"section": before},
            device_id_type=MESH,
        )

    def fold_copy(group):
        return pltpu.make_async_remote_copy(
            src_ref=fold_out.at[group],
            dst_ref=fold_in.at[group],
            send_sem=fold_send.at[group],
            recv_sem=fold_recv.at[group],
            device_id={"section": before},
            device_id_type=MESH,
        )

    def next_copy():
        return pltpu.make_async_remote_copy(
            src_ref=k_hbm.at[0],
            dst_ref=next_keys,
            send_sem=next_sem.at[0],
            recv_sem=next_sem.at[1],
            device_id={"section": before},
            device_id_type=MESH,
        )

    def aside_copy(group, which):
        return pltpu.make_async_remote_copy(
            src_ref=final.at[group, which],
            dst_ref=aside.at[group, which],
            send_sem=final_send.at[which, group],
            recv_sem=aside_recv.at[which, group],
            device_id={"ctx": 0},
            device_id_type=MESH,
        )

    def detour_copy(group, which):
        return pltpu.make_async_remote_copy(
            src_ref=aside.at[group, which],
            dst_ref=relay.at[group, which],
            send_sem=aside_send.at[which, group],
            recv_sem=relay_recv.at[which, group],
            device_id={"section": before},
            device_id_type=MESH,
        )

    def relay_copy(group, which):
        return pltpu.make_async_remote_copy(
            src_ref=relay.at[group, which],
            dst_ref=(out_k, out_v)[which].at[0, :, cols(group)],
            send_sem=relay_send.at[which, group],
            recv_sem=out_recv.at[1 + which],
            device_id={"ctx": last},
            device_id_type=MESH,
        )

    def final_copy(group, which):
        return pltpu.make_async_remote_copy(
            src_ref=final.at[group, which],
            dst_ref=(out_k, out_v)[which].at[0, :, cols(group)],
            send_sem=final_send.at[which, group],
            recv_sem=out_recv.at[1 + which],
            device_id={"section": before},
            device_id_type=MESH,
        )

    def fill_bias(key_blocks):
        for low in range(blocks_here):
            query_block = ctx * blocks_here + low
            position = query_block * BLK + lax.broadcasted_iota(jnp.int32, (BLK, BLK), 0)
            for key_block in range(key_blocks):
                listed = jnp.int32(0)
                for entry in range(block_total):
                    hit = (list_ref[0, query_block, entry] == key_block) & (
                        entry < count_ref[0, query_block]
                    )
                    listed = listed | hit.astype(jnp.int32)
                key_place = key_block * BLK + lax.broadcasted_iota(jnp.int32, (BLK, BLK), 1)
                end = end_ref[:, key_block * BLK : (key_block + 1) * BLK] * listed
                allowed = (key_place <= position) & (position < end)
                bias[
                    key_block * BLK : (key_block + 1) * BLK, low * BLK : (low + 1) * BLK
                ] = jnp.where(allowed, 0.0, -jnp.inf).astype(F32).T

    def corner():
        down = lax.broadcasted_iota(jnp.int32, (rows, rows), 0)
        across = lax.broadcasted_iota(jnp.int32, (rows, rows), 1)
        return down, across

    def fold(group, score_float):
        down, across = corner()
        place = lax.broadcasted_iota(jnp.int32, (DIAG, rows), 0)
        diagonals = jnp.zeros((DIAG, rows), F32)
        for pair in range(FOLDS):
            upper = score_float[:, 2 * pair * rows : (2 * pair + 1) * rows]
            other = score_float[:, (2 * pair + 1) * rows : (2 * pair + 2) * rows]
            square = jnp.where(down <= across, upper, other.T)
            fold_out[group, pair * rows : (pair + 1) * rows, :] = square.astype(BF16)
            diagonal = jnp.sum(jnp.where(down == across, other, 0.0), axis=0, keepdims=True)
            diagonals = jnp.where(place == pair, diagonal, diagonals)
        fold_out[group, FOLDS * rows :, :] = diagonals.astype(BF16)

    def unfold(group):
        down, across = corner()
        keys = next_keys[:, cols(group)]
        diagonals = fold_in[group, FOLDS * rows :, :].astype(F32)
        uppers, lowers = [], []
        for pair in range(FOLDS):
            square = fold_in[group, pair * rows : (pair + 1) * rows, :].astype(F32)
            diagonal = diagonals[pair : pair + 1, :]
            uppers.append(jnp.where(down <= across, square, 0.0).astype(BF16))
            rest = jnp.where(down == across, diagonal, 0.0)
            lowers.append(jnp.where(down > across, square, rest).astype(BF16))
        even = contract(jnp.concatenate(uppers, axis=1), keys, 0, 0).astype(BF16)
        odd = contract(jnp.concatenate(lowers, axis=0), keys, 1, 0).astype(BF16)
        for pair in range(FOLDS):
            here = slice(pair * rows, (pair + 1) * rows)
            out_q[0, :, cols(group * RATIO + 2 * pair)] = even[here]
            out_q[0, :, cols(group * RATIO + 2 * pair + 1)] = odd[here]

    def run(mine):
        length = (mine + 1) * rows
        def send_keys(group):
            for peer in range(mine + 1, ctx_total):
                for which in range(2):
                    kv_copy(group, which, mine, peer).start()

        def enter():
            @pl.when(section % 2 == 0)
            def _():
                if ctx_total > 1:
                    pl.semaphore_wait(barrier, ctx_total - 1)

            @pl.when(section % 2 == 1)
            def _():
                pl.semaphore_wait(barrier, ctx_total + 1)
                pl.semaphore_signal(ready, 1, device_id={"section": after}, device_id_type=MESH)

        def reach():
            pl.when(section % 2 == 0)(lambda: pl.semaphore_wait(ready, 1))
            if mine == 0:
                next_copy().start()

        def wait_own(group):
            pltpu.make_async_copy(
                kv_buf.at[group, :, pl.ds(mine * rows, rows)],
                kv_buf.at[group, :, pl.ds(mine * rows, rows)],
                kv_sem.at[group],
            ).wait()

        def lead(group):
            if mine < last:
                pl.when(section % 2 == 0)(lambda: send_keys(group))

        late = 0 < mine == last
        enter()
        if not late:
            lead(0)
        for table in tables:
            table.wait()
        fill_bias((mine + 1) * blocks_here)
        pl.loop(1, KV_HEADS)(load)
        if mine == 0:
            pl.when(section > 0)(reach)
        heads = RATIO if mine == 0 else PAIR
        span = heads * rows

        def per_group(group, carry):
            wait_own(group)
            if not late:
                pl.when(group > 0)(lambda: lead(group))
            if mine < last:
                pl.when((section % 2 == 1) & (group > 0))(lambda: send_keys(group - 1))
            for source in range(mine):
                pltpu.make_async_copy(
                    kv_buf.at[group, :, pl.ds(source * rows, rows)],
                    kv_buf.at[group, :, pl.ds(source * rows, rows)],
                    kv_recv.at[source, group],
                ).wait()
            pltpu.make_async_copy(q_buf.at[group], q_buf.at[group], load_sem.at[0, group]).wait()
            pltpu.make_async_copy(g_buf.at[group], g_buf.at[group], load_sem.at[1, group]).wait()
            keys = kv_buf[group, 0, 0:length, :]
            values = kv_buf[group, 1, 0:length, :]

            def stacked(ref, first, count):
                parts = [ref[group, :, cols(first + low)] for low in range(count)]
                return jnp.concatenate(parts, axis=0)

            def per_pair(pair):
                here = slice(pair * span, pair * span + span)
                scores = contract(keys, stacked(q_buf, pair * heads, heads), 1, 1)
                masked = bias[0:length, :]
                scores = scores + jnp.concatenate([masked] * heads, axis=1)
                shifted = scores - jnp.max(scores, axis=0, keepdims=True)
                exponent = jnp.exp2(shifted * (scale * math.log2(math.e)))
                total = jnp.sum(exponent, axis=0, keepdims=True)
                attention = exponent * (1.0 / total)
                at_buf[0:length, here] = attention.astype(BF16)
                weight_grad = contract(values, stacked(g_buf, pair * heads, heads), 1, 1)
                row_delta = jnp.sum(attention * weight_grad, axis=0, keepdims=True)
                score_float = attention * (weight_grad - row_delta) * scale
                score_grad = score_float.astype(BF16)
                ds_buf[0:length, here] = score_grad
                if mine == 0:
                    fold(group, score_float)
                    pl.when((group == 0) & (section == 0))(reach)
                    fold_copy(group).start()
                    return
                query_grad = contract(score_grad, keys, 0, 0).astype(BF16)
                for low in range(heads):
                    dq_buf[group, :, cols(pair * heads + low)] = query_grad[low * rows : (low + 1) * rows]
                if mine > 0 and pair == 0:
                    pl.when(group == 0)(reach)
                query_copy(group, pair).start()

            for pair in range(RATIO // heads):
                per_pair(pair)
            key_grad = contract(ds_buf[0:length, :], stacked(q_buf, 0, RATIO), 1, 0)
            value_grad = contract(at_buf[0:length, :], stacked(g_buf, 0, RATIO), 1, 0)
            first = mine * rows
            if mine == last:
                final[group, 0] = key_grad[first:].astype(BF16)
                final[group, 1] = value_grad[first:].astype(BF16)
                for which in range(2):
                    if mine > 0:
                        by_side = detoured(section, group)
                        pl.when(by_side)(aside_copy(group, which).start)
                        pl.when(jnp.logical_not(by_side))(final_copy(group, which).start)
                    else:
                        final_copy(group, which).start()
            else:
                own[group, 0] = key_grad[first:]
                own[group, 1] = value_grad[first:]
            if mine > 0:
                share[group, 0, 0:first, :] = key_grad[0:first].astype(BF16)
                share[group, 1, 0:first, :] = value_grad[0:first].astype(BF16)
                for peer in range(mine):
                    share_copy(group, mine, peer).start()
            return carry

        lax.fori_loop(0, KV_HEADS, per_group, 0)
        if mine < last:
            pl.when(section % 2 == 1)(lambda: send_keys(KV_HEADS - 1))

        if mine == 0:
            next_copy().wait_recv()

        def forward(group):
            for which in range(2):
                aside_copy(group, which).wait_recv()
                detour_copy(group, which).start()

        def hand_over(group):
            for which in range(2):
                detour_copy(group, which).wait_recv()
                relay_copy(group, which).start()

        def finish(group):
            if mine == 0:
                fold_copy(group).wait_recv()
                unfold(group)
            if mine < last:
                total = own[group]
                for source in range(mine + 1, ctx_total):
                    share_copy(group, source, mine).wait_recv()
                    total = total + shares_in[group, source].astype(F32)
                final[group] = total.astype(BF16)
                for which in range(2):
                    final_copy(group, which).start()
            if mine == 0 and last > 0:
                pl.when(detoured(section, group))(lambda: forward(group))
                handed = (group > 0) & detoured(after, group - 1)
                pl.when(handed)(lambda: hand_over(group - 1))

        if mine < last or mine == 0:
            pl.loop(0, KV_HEADS)(finish)

        @pl.loop(0, KV_HEADS)
        def _(group):
            for peer in range(mine + 1, ctx_total):
                for which in range(2):
                    kv_copy(group, which, mine, peer).wait_send()
            for peer in range(mine):
                share_copy(group, mine, peer).wait_send()
            for which in range(2):
                final_copy(group, which).wait_send()
            if mine > 0:
                pltpu.make_async_copy(dq_buf.at[group], dq_buf.at[group], dq_send.at[group]).wait()
            else:
                fold_copy(group).wait_send()
            if mine == 0 and last > 0:

                @pl.when(detoured(after, group))
                def _():
                    for which in range(2):
                        relay_copy(group, which).wait_send()

                @pl.when(detoured(section, group))
                def _():
                    for which in range(2):
                        detour_copy(group, which).wait_send()

        if mine == 0:
            next_copy().wait_send()
        else:
            pltpu.make_async_copy(out_q, out_q, out_recv.at[0]).wait()

    for mine in range(ctx_total):
        pl.when(ctx == mine)(functools.partial(run, mine))

    for slot, out in ((1, out_k), (2, out_v)):
        pltpu.make_async_copy(out, out, out_recv.at[slot]).wait()


def write_out(held_q, held_k, held_v, out_q, out_k, out_v, done):
    pairs = ((held_q, out_q), (held_k, out_k), (held_v, out_v))
    copies = [pltpu.make_async_copy(a, b, done.at[slot]) for slot, (a, b) in enumerate(pairs)]
    for copy in copies:
        copy.start()
    for copy in copies:
        copy.wait()


def per_device(
    section_total,
    ctx_total,
    queries,
    key_states,
    value_states,
    out_grad,
    node_end,
    block_list,
    block_count,
):
    rows = queries.shape[1]
    length = node_end.shape[1]
    anywhere = pl.BlockSpec(memory_space=pl.ANY)
    vector = pl.BlockSpec(memory_space=pltpu.VMEM)
    dma = pltpu.SemaphoreType.DMA
    tall = RATIO * rows
    held = pl.pallas_call(
        functools.partial(kernel, section_total, ctx_total),
        out_shape=(
            pltpu.VMEM(queries.shape, BF16),
            pltpu.VMEM(key_states.shape, BF16),
            pltpu.VMEM(value_states.shape, BF16),
        ),
        in_specs=[anywhere] * 7,
        out_specs=[vector] * 3,
        scratch_shapes=[
            pltpu.VMEM((KV_HEADS, rows, WIDTH), BF16),
            pltpu.VMEM((KV_HEADS, rows, WIDTH), BF16),
            pltpu.VMEM((KV_HEADS, 2, length, HEAD_DIM), BF16),
            pltpu.VMEM((KV_HEADS, rows, WIDTH), BF16),
            pltpu.VMEM((length, tall), BF16),
            pltpu.VMEM((length, tall), BF16),
            pltpu.VMEM((length, rows), F32),
            pltpu.VMEM((KV_HEADS, 2, rows, HEAD_DIM), F32),
            pltpu.VMEM((KV_HEADS, 2, length, HEAD_DIM), BF16),
            pltpu.VMEM((KV_HEADS, ctx_total, 2, rows, HEAD_DIM), BF16),
            pltpu.VMEM((KV_HEADS, 2, rows, HEAD_DIM), BF16),
            pltpu.VMEM((KV_HEADS, FOLDS * rows + DIAG, rows), BF16),
            pltpu.VMEM((KV_HEADS, FOLDS * rows + DIAG, rows), BF16),
            pltpu.VMEM((rows, KV_HEADS * HEAD_DIM), BF16),
            pltpu.VMEM((KV_HEADS, 2, rows, HEAD_DIM), BF16),
            pltpu.VMEM((KV_HEADS, 2, rows, HEAD_DIM), BF16),
            pltpu.VMEM(node_end.shape, jnp.int32),
            pltpu.SMEM(block_list.shape, jnp.int32),
            pltpu.SMEM(block_count.shape, jnp.int32),
            dma((3,)),
            dma((2, KV_HEADS)),
            dma((KV_HEADS,)),
            dma((ctx_total, KV_HEADS, 2)),
            dma((ctx_total, KV_HEADS)),
            dma((KV_HEADS,)),
            dma((ctx_total, KV_HEADS)),
            dma((ctx_total, KV_HEADS)),
            dma((2, KV_HEADS)),
            dma((3,)),
            dma((KV_HEADS,)),
            dma((KV_HEADS,)),
            dma((2,)),
            dma((2, KV_HEADS)),
            dma((2, KV_HEADS)),
            dma((2, KV_HEADS)),
            dma((2, KV_HEADS)),
            pltpu.SemaphoreType.REGULAR,
        ],
        compiler_params=pltpu.CompilerParams(collective_id=0, has_side_effects=True),
    )(queries, key_states, value_states, out_grad, node_end, block_list, block_count)
    return pl.pallas_call(
        write_out,
        out_shape=tuple(jax.ShapeDtypeStruct(part.shape, BF16) for part in held),
        in_specs=[anywhere] * 3,
        out_specs=[anywhere] * 3,
        scratch_shapes=[dma((len(held),))],
        compiler_params=pltpu.CompilerParams(vmem_limit_bytes=1 << 20),
    )(*held)


def solution(mesh):
    wide = P("section", "ctx", None)
    return jax.shard_map(
        functools.partial(per_device, mesh.shape["section"], mesh.shape["ctx"]),
        mesh=mesh,
        in_specs=(wide, wide, wide, wide, P("section", None), P("section", None, None), P("section", None)),
        out_specs=(wide, wide, wide),
        check_vma=False,
    )
```

```python
import functools
import math

import jax
import jax.numpy as jnp
from jax import lax
from jax.experimental import pallas as pl
from jax.experimental.pallas import tpu as pltpu
from jax.sharding import PartitionSpec as P

HEADS = 64
KV_HEADS = 8
HEAD_DIM = 128
BLK = 128
RATIO = HEADS // KV_HEADS
STEPS = (4, 4)
FIRST_STEPS = (2, 2, 4)
WIDTH = RATIO * HEAD_DIM
FOLDS = RATIO // 2
DIAG = 16
DIRECT = 1
DIRECT_WRAP = 2

F32 = jnp.float32
BF16 = jnp.bfloat16
MESH = pl.DeviceIdType.MESH


def contract(left, right, left_dim, right_dim):
    return lax.dot_general(
        left, right, (((left_dim,), (right_dim,)), ((), ())), preferred_element_type=F32
    )


def kernel(
    section_total,
    ctx_total,
    q_hbm,
    k_hbm,
    v_hbm,
    g_hbm,
    end_hbm,
    list_hbm,
    count_hbm,
    out_q,
    out_k,
    out_v,
    q_buf,
    g_buf,
    kv_buf,
    dq_buf,
    ds_buf,
    at_buf,
    bias,
    own,
    share,
    shares_in,
    final,
    fold_out,
    fold_in,
    next_keys,
    aside,
    relay,
    end_ref,
    list_ref,
    count_ref,
    table_sem,
    load_sem,
    kv_sem,
    kv_send,
    kv_recv,
    dq_send,
    share_send,
    share_recv,
    final_send,
    out_recv,
    fold_send,
    fold_recv,
    next_sem,
    aside_send,
    aside_recv,
    relay_send,
    relay_recv,
    ready,
):
    rows = q_hbm.shape[1]
    block_total = list_hbm.shape[1]
    blocks_here = rows // BLK
    scale = 1.0 / math.sqrt(HEAD_DIM)
    last = ctx_total - 1
    section = lax.axis_index("section")
    ctx = lax.axis_index("ctx")
    before = lax.rem(section + section_total - 1, section_total)
    after = lax.rem(section + 1, section_total)

    def detoured(source, group):
        direct = jnp.where(source == 0, DIRECT_WRAP, DIRECT)
        return (source % 2 == 0) & (group < KV_HEADS - direct)

    def cols(index, width=HEAD_DIM):
        if isinstance(index, int):
            return slice(index * width, index * width + width)
        return pl.ds(pl.multiple_of(index * width, width), width)

    def block(index):
        return pl.ds(pl.multiple_of(index * rows, rows), rows)

    barrier = pltpu.get_barrier_semaphore()

    @pl.when(section % 2 == 0)
    def _():
        for target in (before, after):
            pl.semaphore_signal(barrier, 1, device_id={"section": target}, device_id_type=MESH)

    for step in range(1, ctx_total):
        other = lax.rem(ctx + step, ctx_total)
        pl.semaphore_signal(barrier, 1, device_id={"ctx": other}, device_id_type=MESH)
    def load(group):
        for which, source in enumerate((k_hbm, v_hbm)):
            pltpu.make_async_copy(
                source.at[0, :, cols(group)], kv_buf.at[group, which, block(ctx)], kv_sem.at[group]
            ).start()
        for which, (source, target) in enumerate(((q_hbm, q_buf), (g_hbm, g_buf))):
            pltpu.make_async_copy(
                source.at[0, :, cols(group, WIDTH)], target.at[group], load_sem.at[which, group]
            ).start()

    tables = [
        pltpu.make_async_copy(source, target, table_sem.at[slot])
        for slot, (source, target) in enumerate(
            ((end_hbm, end_ref), (list_hbm, list_ref), (count_hbm, count_ref))
        )
    ]
    for table in tables:
        table.start()
    load(0)

    def kv_copy(group, which, source, peer):
        return pltpu.make_async_remote_copy(
            src_ref=(k_hbm, v_hbm)[which].at[0, :, cols(group)],
            dst_ref=kv_buf.at[group, which, block(source)],
            send_sem=kv_send.at[peer, group, which],
            recv_sem=kv_recv.at[source, group],
            device_id={"ctx": peer},
            device_id_type=MESH,
        )

    def share_copy(group, source, peer):
        return pltpu.make_async_remote_copy(
            src_ref=share.at[group, :, pl.ds(peer * rows, rows)],
            dst_ref=shares_in.at[group, source],
            send_sem=share_send.at[peer, group],
            recv_sem=share_recv.at[source, group],
            device_id={"ctx": peer},
            device_id_type=MESH,
        )

    def query_copy(group, first, count):
        start = group * WIDTH + first * HEAD_DIM
        if not isinstance(group, int):
            start = pl.multiple_of(start, HEAD_DIM)
        return pltpu.make_async_remote_copy(
            src_ref=dq_buf.at[group, :, first * HEAD_DIM : (first + count) * HEAD_DIM],
            dst_ref=out_q.at[0, :, pl.ds(start, count * HEAD_DIM)],
            send_sem=dq_send.at[group],
            recv_sem=out_recv.at[0],
            device_id={"section": before},
            device_id_type=MESH,
        )

    def fold_copy(group):
        return pltpu.make_async_remote_copy(
            src_ref=fold_out.at[group],
            dst_ref=fold_in.at[group],
            send_sem=fold_send.at[group],
            recv_sem=fold_recv.at[group],
            device_id={"section": before},
            device_id_type=MESH,
        )

    def next_copy():
        return pltpu.make_async_remote_copy(
            src_ref=k_hbm.at[0],
            dst_ref=next_keys,
            send_sem=next_sem.at[0],
            recv_sem=next_sem.at[1],
            device_id={"section": before},
            device_id_type=MESH,
        )

    def aside_copy(group, which):
        return pltpu.make_async_remote_copy(
            src_ref=final.at[group, which],
            dst_ref=aside.at[group, which],
            send_sem=final_send.at[which, group],
            recv_sem=aside_recv.at[which, group],
            device_id={"ctx": 0},
            device_id_type=MESH,
        )

    def detour_copy(group, which):
        return pltpu.make_async_remote_copy(
            src_ref=aside.at[group, which],
            dst_ref=relay.at[group, which],
            send_sem=aside_send.at[which, group],
            recv_sem=relay_recv.at[which, group],
            device_id={"section": before},
            device_id_type=MESH,
        )

    def relay_copy(group, which):
        return pltpu.make_async_remote_copy(
            src_ref=relay.at[group, which],
            dst_ref=(out_k, out_v)[which].at[0, :, cols(group)],
            send_sem=relay_send.at[which, group],
            recv_sem=out_recv.at[1 + which],
            device_id={"ctx": last},
            device_id_type=MESH,
        )

    def final_copy(group, which):
        return pltpu.make_async_remote_copy(
            src_ref=final.at[group, which],
            dst_ref=(out_k, out_v)[which].at[0, :, cols(group)],
            send_sem=final_send.at[which, group],
            recv_sem=out_recv.at[1 + which],
            device_id={"section": before},
            device_id_type=MESH,
        )

    def fill_bias(key_blocks):
        for low in range(blocks_here):
            query_block = ctx * blocks_here + low
            position = query_block * BLK + lax.broadcasted_iota(jnp.int32, (BLK, BLK), 0)
            for key_block in range(key_blocks):
                listed = jnp.int32(0)
                for entry in range(block_total):
                    hit = (list_ref[0, query_block, entry] == key_block) & (
                        entry < count_ref[0, query_block]
                    )
                    listed = listed | hit.astype(jnp.int32)
                key_place = key_block * BLK + lax.broadcasted_iota(jnp.int32, (BLK, BLK), 1)
                end = end_ref[:, key_block * BLK : (key_block + 1) * BLK] * listed
                allowed = (key_place <= position) & (position < end)
                bias[
                    key_block * BLK : (key_block + 1) * BLK, low * BLK : (low + 1) * BLK
                ] = jnp.where(allowed, 0.0, -jnp.inf).astype(F32).T

    def corner():
        down = lax.broadcasted_iota(jnp.int32, (rows, rows), 0)
        across = lax.broadcasted_iota(jnp.int32, (rows, rows), 1)
        return down, across

    def fold(group, score_float):
        down, across = corner()
        place = lax.broadcasted_iota(jnp.int32, (DIAG, rows), 0)
        diagonals = jnp.zeros((DIAG, rows), F32)
        for pair in range(FOLDS):
            upper = score_float[:, 2 * pair * rows : (2 * pair + 1) * rows]
            other = score_float[:, (2 * pair + 1) * rows : (2 * pair + 2) * rows]
            square = jnp.where(down <= across, upper, other.T)
            fold_out[group, pair * rows : (pair + 1) * rows, :] = square.astype(BF16)
            diagonal = jnp.sum(jnp.where(down == across, other, 0.0), axis=0, keepdims=True)
            diagonals = jnp.where(place == pair, diagonal, diagonals)
        fold_out[group, FOLDS * rows :, :] = diagonals.astype(BF16)

    def unfold(group):
        down, across = corner()
        keys = next_keys[:, cols(group)]
        diagonals = fold_in[group, FOLDS * rows :, :].astype(F32)
        uppers, lowers = [], []
        for pair in range(FOLDS):
            square = fold_in[group, pair * rows : (pair + 1) * rows, :].astype(F32)
            diagonal = diagonals[pair : pair + 1, :]
            uppers.append(jnp.where(down <= across, square, 0.0).astype(BF16))
            rest = jnp.where(down == across, diagonal, 0.0)
            lowers.append(jnp.where(down > across, square, rest).astype(BF16))
        even = contract(jnp.concatenate(uppers, axis=1), keys, 0, 0).astype(BF16)
        odd = contract(jnp.concatenate(lowers, axis=0), keys, 1, 0).astype(BF16)
        for pair in range(FOLDS):
            here = slice(pair * rows, (pair + 1) * rows)
            out_q[0, :, cols(group * RATIO + 2 * pair)] = even[here]
            out_q[0, :, cols(group * RATIO + 2 * pair + 1)] = odd[here]

    def run(mine):
        length = (mine + 1) * rows
        def send_keys(group):
            for peer in range(mine + 1, ctx_total):
                for which in range(2):
                    kv_copy(group, which, mine, peer).start()

        def enter():
            @pl.when(section % 2 == 0)
            def _():
                if ctx_total > 1:
                    pl.semaphore_wait(barrier, ctx_total - 1)

            @pl.when(section % 2 == 1)
            def _():
                pl.semaphore_wait(barrier, ctx_total + 1)
                pl.semaphore_signal(ready, 1, device_id={"section": after}, device_id_type=MESH)

        def when_first(group, action):
            if not isinstance(group, int):
                pl.when(group == 0)(action)
            elif group == 0:
                action()

        def reach():
            pl.when(section % 2 == 0)(lambda: pl.semaphore_wait(ready, 1))
            if mine == 0:
                next_copy().start()

        def wait_own(group):
            pltpu.make_async_copy(
                kv_buf.at[group, :, pl.ds(mine * rows, rows)],
                kv_buf.at[group, :, pl.ds(mine * rows, rows)],
                kv_sem.at[group],
            ).wait()

        def lead(group):
            if mine < last:
                pl.when(section % 2 == 0)(lambda: send_keys(group))

        late = 0 < mine == last
        enter()
        if not late:
            lead(0)
        for table in tables:
            table.wait()
        fill_bias((mine + 1) * blocks_here)
        pl.loop(1, KV_HEADS)(load)
        if mine == 0:
            pl.when(section > 0)(reach)
        usual = (RATIO,) if mine == 0 else STEPS

        def per_group(group, carry, steps=usual):
            wait_own(group)
            if not late:
                pl.when(group > 0)(lambda: lead(group))
            if mine < last:
                pl.when((section % 2 == 1) & (group > 0))(lambda: send_keys(group - 1))
            for source in range(mine):
                pltpu.make_async_copy(
                    kv_buf.at[group, :, pl.ds(source * rows, rows)],
                    kv_buf.at[group, :, pl.ds(source * rows, rows)],
                    kv_recv.at[source, group],
                ).wait()
            pltpu.make_async_copy(q_buf.at[group], q_buf.at[group], load_sem.at[0, group]).wait()
            pltpu.make_async_copy(g_buf.at[group], g_buf.at[group], load_sem.at[1, group]).wait()
            keys = kv_buf[group, 0, 0:length, :]
            values = kv_buf[group, 1, 0:length, :]

            def stacked(ref, first, count):
                parts = [ref[group, :, cols(first + low)] for low in range(count)]
                return jnp.concatenate(parts, axis=0)

            def per_step(start, heads):
                here = slice(start * rows, (start + heads) * rows)
                scores = contract(keys, stacked(q_buf, start, heads), 1, 1)
                masked = bias[0:length, :]
                scores = scores + jnp.concatenate([masked] * heads, axis=1)
                shifted = scores - jnp.max(scores, axis=0, keepdims=True)
                exponent = jnp.exp2(shifted * (scale * math.log2(math.e)))
                total = jnp.sum(exponent, axis=0, keepdims=True)
                attention = exponent * (1.0 / total)
                at_buf[0:length, here] = attention.astype(BF16)
                weight_grad = contract(values, stacked(g_buf, start, heads), 1, 1)
                row_delta = jnp.sum(attention * weight_grad, axis=0, keepdims=True)
                score_float = attention * (weight_grad - row_delta) * scale
                score_grad = score_float.astype(BF16)
                ds_buf[0:length, here] = score_grad
                if mine == 0:
                    fold(group, score_float)
                    pl.when((group == 0) & (section == 0))(reach)
                    fold_copy(group).start()
                    return
                query_grad = contract(score_grad, keys, 0, 0).astype(BF16)
                for low in range(heads):
                    dq_buf[group, :, cols(start + low)] = query_grad[low * rows : (low + 1) * rows]
                if mine > 0 and start == 0:
                    when_first(group, reach)
                query_copy(group, start, heads).start()

            for step, heads in enumerate(steps):
                per_step(sum(steps[:step]), heads)
            key_grad = contract(ds_buf[0:length, :], stacked(q_buf, 0, RATIO), 1, 0)
            value_grad = contract(at_buf[0:length, :], stacked(g_buf, 0, RATIO), 1, 0)
            first = mine * rows
            if mine == last:
                final[group, 0] = key_grad[first:].astype(BF16)
                final[group, 1] = value_grad[first:].astype(BF16)
                for which in range(2):
                    if mine > 0:
                        by_side = detoured(section, group)
                        pl.when(by_side)(aside_copy(group, which).start)
                        pl.when(jnp.logical_not(by_side))(final_copy(group, which).start)
                    else:
                        final_copy(group, which).start()
            else:
                own[group, 0] = key_grad[first:]
                own[group, 1] = value_grad[first:]
            if mine > 0:
                share[group, 0, 0:first, :] = key_grad[0:first].astype(BF16)
                share[group, 1, 0:first, :] = value_grad[0:first].astype(BF16)
                for peer in range(mine):
                    share_copy(group, mine, peer).start()
            return carry

        if late:
            per_group(0, 0, FIRST_STEPS)
        lax.fori_loop(int(late), KV_HEADS, per_group, 0)
        if mine < last:
            pl.when(section % 2 == 1)(lambda: send_keys(KV_HEADS - 1))

        if mine == 0:
            next_copy().wait_recv()

        def forward(group):
            for which in range(2):
                aside_copy(group, which).wait_recv()
                detour_copy(group, which).start()

        def hand_over(group):
            for which in range(2):
                detour_copy(group, which).wait_recv()
                relay_copy(group, which).start()

        def finish(group):
            if mine == 0:
                fold_copy(group).wait_recv()
                unfold(group)
            if mine < last:
                total = own[group]
                for source in range(mine + 1, ctx_total):
                    share_copy(group, source, mine).wait_recv()
                    total = total + shares_in[group, source].astype(F32)
                final[group] = total.astype(BF16)
                for which in range(2):
                    final_copy(group, which).start()
            if mine == 0 and last > 0:
                pl.when(detoured(section, group))(lambda: forward(group))
                handed = (group > 0) & detoured(after, group - 1)
                pl.when(handed)(lambda: hand_over(group - 1))

        if mine < last or mine == 0:
            pl.loop(0, KV_HEADS)(finish)

        @pl.loop(0, KV_HEADS)
        def _(group):
            for peer in range(mine + 1, ctx_total):
                for which in range(2):
                    kv_copy(group, which, mine, peer).wait_send()
            for peer in range(mine):
                share_copy(group, mine, peer).wait_send()
            for which in range(2):
                final_copy(group, which).wait_send()
            if mine > 0:
                pltpu.make_async_copy(dq_buf.at[group], dq_buf.at[group], dq_send.at[group]).wait()
            else:
                fold_copy(group).wait_send()
            if mine == 0 and last > 0:

                @pl.when(detoured(after, group))
                def _():
                    for which in range(2):
                        relay_copy(group, which).wait_send()

                @pl.when(detoured(section, group))
                def _():
                    for which in range(2):
                        detour_copy(group, which).wait_send()

        if mine == 0:
            next_copy().wait_send()
        else:
            pltpu.make_async_copy(out_q, out_q, out_recv.at[0]).wait()

    for mine in range(ctx_total):
        pl.when(ctx == mine)(functools.partial(run, mine))

    for slot, out in ((1, out_k), (2, out_v)):
        pltpu.make_async_copy(out, out, out_recv.at[slot]).wait()


def write_out(held_q, held_k, held_v, out_q, out_k, out_v, done):
    pairs = ((held_q, out_q), (held_k, out_k), (held_v, out_v))
    copies = [pltpu.make_async_copy(a, b, done.at[slot]) for slot, (a, b) in enumerate(pairs)]
    for copy in copies:
        copy.start()
    for copy in copies:
        copy.wait()


def per_device(
    section_total,
    ctx_total,
    queries,
    key_states,
    value_states,
    out_grad,
    node_end,
    block_list,
    block_count,
):
    rows = queries.shape[1]
    length = node_end.shape[1]
    anywhere = pl.BlockSpec(memory_space=pl.ANY)
    vector = pl.BlockSpec(memory_space=pltpu.VMEM)
    dma = pltpu.SemaphoreType.DMA
    tall = RATIO * rows
    held = pl.pallas_call(
        functools.partial(kernel, section_total, ctx_total),
        out_shape=(
            pltpu.VMEM(queries.shape, BF16),
            pltpu.VMEM(key_states.shape, BF16),
            pltpu.VMEM(value_states.shape, BF16),
        ),
        in_specs=[anywhere] * 7,
        out_specs=[vector] * 3,
        scratch_shapes=[
            pltpu.VMEM((KV_HEADS, rows, WIDTH), BF16),
            pltpu.VMEM((KV_HEADS, rows, WIDTH), BF16),
            pltpu.VMEM((KV_HEADS, 2, length, HEAD_DIM), BF16),
            pltpu.VMEM((KV_HEADS, rows, WIDTH), BF16),
            pltpu.VMEM((length, tall), BF16),
            pltpu.VMEM((length, tall), BF16),
            pltpu.VMEM((length, rows), F32),
            pltpu.VMEM((KV_HEADS, 2, rows, HEAD_DIM), F32),
            pltpu.VMEM((KV_HEADS, 2, length, HEAD_DIM), BF16),
            pltpu.VMEM((KV_HEADS, ctx_total, 2, rows, HEAD_DIM), BF16),
            pltpu.VMEM((KV_HEADS, 2, rows, HEAD_DIM), BF16),
            pltpu.VMEM((KV_HEADS, FOLDS * rows + DIAG, rows), BF16),
            pltpu.VMEM((KV_HEADS, FOLDS * rows + DIAG, rows), BF16),
            pltpu.VMEM((rows, KV_HEADS * HEAD_DIM), BF16),
            pltpu.VMEM((KV_HEADS, 2, rows, HEAD_DIM), BF16),
            pltpu.VMEM((KV_HEADS, 2, rows, HEAD_DIM), BF16),
            pltpu.VMEM(node_end.shape, jnp.int32),
            pltpu.SMEM(block_list.shape, jnp.int32),
            pltpu.SMEM(block_count.shape, jnp.int32),
            dma((3,)),
            dma((2, KV_HEADS)),
            dma((KV_HEADS,)),
            dma((ctx_total, KV_HEADS, 2)),
            dma((ctx_total, KV_HEADS)),
            dma((KV_HEADS,)),
            dma((ctx_total, KV_HEADS)),
            dma((ctx_total, KV_HEADS)),
            dma((2, KV_HEADS)),
            dma((3,)),
            dma((KV_HEADS,)),
            dma((KV_HEADS,)),
            dma((2,)),
            dma((2, KV_HEADS)),
            dma((2, KV_HEADS)),
            dma((2, KV_HEADS)),
            dma((2, KV_HEADS)),
            pltpu.SemaphoreType.REGULAR,
        ],
        compiler_params=pltpu.CompilerParams(collective_id=0, has_side_effects=True),
    )(queries, key_states, value_states, out_grad, node_end, block_list, block_count)
    return pl.pallas_call(
        write_out,
        out_shape=tuple(jax.ShapeDtypeStruct(part.shape, BF16) for part in held),
        in_specs=[anywhere] * 3,
        out_specs=[anywhere] * 3,
        scratch_shapes=[dma((len(held),))],
        compiler_params=pltpu.CompilerParams(vmem_limit_bytes=1 << 20),
    )(*held)


def solution(mesh):
    wide = P("section", "ctx", None)
    return jax.shard_map(
        functools.partial(per_device, mesh.shape["section"], mesh.shape["ctx"]),
        mesh=mesh,
        in_specs=(wide, wide, wide, wide, P("section", None), P("section", None, None), P("section", None)),
        out_specs=(wide, wide, wide),
        check_vma=False,
    )
```
